512 devices in a mesh: seq: 32 (over z_hi, y), tensor: 8 (over x, z_lo), group: 2 (over core).
Axes of the slice: x: 4, y: 8, z: 8 (z_hi: 4, z_lo: 2; z = z_hi * 2 + z_lo), core: 2. Of those that a mesh axis runs over, the one named last changes fastest.
Arguments:
- prefill_queries: bfloat16 [512, 8192], P(None, 'tensor'), may hold values from -6 to 6
- cached_keys: bfloat16 [65536, 1024], P(('seq', 'group'), 'tensor'), may hold values from -6 to 6
- cached_values: bfloat16 [65536, 1024], P(('seq', 'group'), 'tensor'), may hold values from -6 to 6
- span_keys: bfloat16 [512, 1024], P(('seq', 'group'), 'tensor'), may hold values from -6 to 6
- span_values: bfloat16 [512, 1024], P(('seq', 'group'), 'tensor'), may hold values from -6 to 6
- out_weight: bfloat16 [8192, 8192], P('tensor', 'seq'), may hold values from -0.0625 to 0.0625
- decode_queries: bfloat16 [4, 32, 8192], P(None, 'group', 'tensor'), may hold values from -6 to 6
- decode_keys: bfloat16 [32, 8192, 1024], P('group', 'seq', 'tensor'), may hold values from -6 to 6
- decode_values: bfloat16 [32, 8192, 1024], P('group', 'seq', 'tensor'), may hold values from -6 to 6
- new_keys: bfloat16 [4, 32, 1024], P(None, 'group', 'tensor'), may hold values from -6 to 6
- new_values: bfloat16 [4, 32, 1024], P(None, 'group', 'tensor'), may hold values from -6 to 6
- request_lengths: int32 [32], replicated, may hold values from 1 to 8192
- row_requests: int32 [32], P('group'), may hold values from 0 to 31
- block_table: int32 [128, 1], replicated, may hold values from 0 to 63; in each aligned block of 128 rows (0 to 127, 128 to 255, ...) at most 4 rows name the same one
Outputs:
- prefill_out: bfloat16 [512, 8192], P('group', ('seq', 'tensor'))
- decode_out: bfloat16 [4, 32, 8192], P(None, 'group', ('seq', 'tensor'))
- landed_keys: bfloat16 [64, 4, 4, 1024], P(('seq', 'group'), None, None, 'tensor')
- landed_values: bfloat16 [64, 4, 4, 1024], P(('seq', 'group'), None, None, 'tensor')
The draws below stay inside these ranges and needn't reach their ends.
Inputs may be any that keep to these rules, and one draw needn't show every extreme that they name: `block_table`: each owner receives at most 4 blocks, and some owner receives exactly 4; every owner receives at least one.
All inputs are finite; a program needn't handle non-finite values.
Results may differ from the reference program's by a relative error of at most 0.0052.
Values may be sent and summed in bfloat16 or wider, within the bound.
No kernel may reach another device: no remote copies, remote signals or barrier semaphores. Data moves between devices by JAX's collectives and lax.ppermute only.
A program may use at most 64 MiB of HBM per device.

```python
import math
import jax
import jax.numpy as jnp
import numpy as np
from jax import lax

D = 8192
HEADS = 64
KV_HEADS = 8
HEAD = 128
SPAN = 512
BLOCK = 4
STEPS = 4
CONTEXT = 65536
OWNERS = 64
NBLOCKS = 128
MOST = 4
ROWS = 32
CTX_MAX = 8192
REQUESTS = 32


def base_field(key, shape):
    return jnp.clip(jax.random.normal(key, shape, jnp.float32), -6.0, 6.0)


def aligned_signs(key, salt, count):
    flips = jax.random.bernoulli(jax.random.fold_in(key, salt), 0.5, (count, HEAD))
    return jnp.where(flips, 1.0, -1.0).astype(jnp.float32)


def strength_table(order):
    levels = jnp.array([1.5, 2.0, 3.0, 4.0], jnp.float32)
    return levels[order % 4]


def prefill_plan():
    order = jnp.arange(8, dtype=jnp.int32)
    query_rows = order * (SPAN // 8) + 1
    heads = order * 9 % HEADS
    cached_rows = order * (CONTEXT // 8)
    return (order, query_rows, heads, cached_rows)


def decode_plan():
    count = ROWS // 4
    order = jnp.arange(count, dtype=jnp.int32)
    rows = order * 4
    heads = order * 9 % HEADS
    steps = order % STEPS
    return (order, rows, heads, steps)


def key_pair(signs, order):
    first = strength_table(order)[:, None] * signs
    second = first.at[:, 0].add(-4.0 * signs[:, 0])
    return (first, second)


def draw_prefill_queries(key, part):
    field = base_field(jax.random.fold_in(key, 11), (SPAN, HEADS * HEAD))
    order, query_rows, heads, cached_rows = prefill_plan()
    signs = aligned_signs(key, 4242, 8)
    columns = heads[:, None] * HEAD + jnp.arange(HEAD, dtype=jnp.int32)[None, :]
    field = field.at[query_rows[:, None], columns].set(6.0 * signs)
    return field.astype(jnp.bfloat16)


def draw_cached_keys(key, part):
    field = base_field(jax.random.fold_in(key, 12), (CONTEXT, KV_HEADS * HEAD))
    order, query_rows, heads, cached_rows = prefill_plan()
    signs = aligned_signs(key, 4242, 8)
    first, second = key_pair(signs, order)
    groups = heads // (HEADS // KV_HEADS)
    columns = groups[:, None] * HEAD + jnp.arange(HEAD, dtype=jnp.int32)[None, :]
    field = field.at[cached_rows[:, None], columns].set(first)
    field = field.at[(cached_rows + CONTEXT // 16)[:, None], columns].set(second)
    return field.astype(jnp.bfloat16)


def draw_decode_queries(key, part):
    field = base_field(jax.random.fold_in(key, 13), (STEPS, ROWS, HEADS * HEAD))
    order, rows, heads, steps = decode_plan()
    signs = aligned_signs(key, 4343, ROWS // 4)
    columns = heads[:, None] * HEAD + jnp.arange(HEAD, dtype=jnp.int32)[None, :]
    field = field.at[steps[:, None], rows[:, None], columns].set(6.0 * signs)
    return field.astype(jnp.bfloat16)


def draw_decode_keys(key, part):
    field = base_field(jax.random.fold_in(key, 14), (ROWS, CTX_MAX, KV_HEADS * HEAD))
    order, rows, heads, steps = decode_plan()
    signs = aligned_signs(key, 4343, ROWS // 4)
    first, second = key_pair(signs, order)
    groups = heads // (HEADS // KV_HEADS)
    columns = groups[:, None] * HEAD + jnp.arange(HEAD, dtype=jnp.int32)[None, :]
    field = field.at[rows[:, None], 0, columns].set(first)
    return field.astype(jnp.bfloat16)


def draw_new_keys(key, part):
    field = base_field(jax.random.fold_in(key, 15), (STEPS, ROWS, KV_HEADS * HEAD))
    order, rows, heads, steps = decode_plan()
    signs = aligned_signs(key, 4343, ROWS // 4)
    first, second = key_pair(signs, order)
    groups = heads // (HEADS // KV_HEADS)
    columns = groups[:, None] * HEAD + jnp.arange(HEAD, dtype=jnp.int32)[None, :]
    field = field.at[0, rows[:, None], columns].set(second)
    return field.astype(jnp.bfloat16)


def set_ends(drawn, stream_key, smallest, largest):
    shape = drawn.shape
    place = [jax.random.randint(jax.random.fold_in(stream_key, axis), (), 0, shape[axis]) for axis in range(len(shape))]
    drawn = drawn.at[tuple(place)].set(smallest)
    longest = shape.index(max(shape))
    place[longest] = (place[longest] + 1) % shape[longest]
    return drawn.at[tuple(place)].set(largest)


def shard_levels(key, dims, pieces, least, largest):
    level = 1.0
    for dim, shards_of in pieces:
        heights = jax.random.uniform(jax.random.fold_in(jax.random.fold_in(key, 6), dim), (shards_of,), jnp.float32, least / len(pieces), largest / len(pieces))
        level = level * jnp.repeat(jnp.exp(heights), dims[dim] // shards_of).reshape((-1,) + (1,) * (len(dims) - 1 - dim))
    return level


def deal_out(key, own, number, rows, count, top, reach, skew):
    ranking = jax.random.permutation(key, count)
    crowded, common = shares(count, rows * top, reach, skew, True), shares(count, rows * top, reach, skew, False)
    places = jnp.arange(count)

    def named(sizes, rotation):
        used = int((sizes > 0).sum())
        fixed = max(1, used // 4)
        moved = fixed + (places - fixed + rotation * (used - fixed)) % max(1, count - fixed)
        return jnp.zeros((count,), jnp.int32).at[ranking[jnp.where(places < fixed, places, moved)]].set(jnp.asarray(sizes, jnp.int32))

    sizes = jnp.where(number % 4 == 0, named(crowded, number // 4), named(common, number - number // 4 - 1))
    mixed = jax.random.permutation(jax.random.fold_in(own, 3), count)
    source_of, sink = mixed[0:count // 2 * 2:2], mixed[1:count // 2 * 2:2]
    slack = jnp.minimum(sizes[source_of] - 1, reach - sizes[sink]) // 2
    slack = jnp.where((source_of == ranking[0]) | (sink == ranking[0]) | (sizes[sink] == 0), 0, jnp.maximum(slack, 0))
    moved = jax.random.randint(jax.random.fold_in(own, 4), (count // 2,), 0, 1 << 20) % (slack + 1)
    sizes = sizes.at[source_of].add(-moved).at[sink].add(moved)
    labels = jnp.searchsorted(jnp.cumsum(sizes), jnp.arange(rows * top), side="right").astype(jnp.int32)
    grid = labels.reshape(top, rows).T
    grid = grid[jax.random.permutation(jax.random.fold_in(own, 1), rows)]
    rotation = jax.random.randint(jax.random.fold_in(own, 2), (rows, 1), 0, top)
    return jnp.take_along_axis(grid, (jnp.arange(top)[None, :] + rotation) % top, axis=1)


def shares(count, total, reach, slope, full):
    loads = [(1 << 20) // math.isqrt(rank ** slope) + 1 for rank in range(1, count + 1)]
    largest = reach if full else min(reach, max(-(-total // count), total * loads[0] // sum(loads)))
    least = 1 if total - largest >= count - 1 else 0
    counts, surplus = [largest] + [least] * (count - 1), total - largest - least * (count - 1)
    while surplus > 0:
        movable = [i for i in range(1, count) if counts[i] < largest] or [i for i in range(1, count) if counts[i] < reach]
        whole, left = sum([loads[i] for i in movable]), surplus
        for i in movable:
            extra = min(reach - counts[i], max(1, left * loads[i] // whole), surplus)
            counts[i] = counts[i] + extra
            surplus = surplus - extra
    return np.array(counts)


def noise(rng, extent, spread, reach, split=(), held_as=jnp.bfloat16):
    values = spread * jax.random.normal(rng, extent, jnp.float32)
    if split:
        values = values * shard_levels(rng, extent, split, -0.22, 0.18)
    return jnp.clip(values, -reach, reach).astype(held_as)


def setup_inputs(seed: int = 0) -> dict:
    splits = jax.random.split(jax.random.key(seed), 15)
    prefill_queries = draw_prefill_queries(jax.random.fold_in(splits[14], 71), 0)
    cached_keys = draw_cached_keys(jax.random.fold_in(splits[14], 71), 0)
    cached_values = noise(splits[2], (CONTEXT, KV_HEADS * HEAD), 1.0, 6.0, ((0, 64), (1, 8)))
    span_keys = noise(splits[3], (SPAN, KV_HEADS * HEAD), 1.0, 6.0, ((0, 64), (1, 8)))
    span_values = noise(splits[4], (SPAN, KV_HEADS * HEAD), 1.0, 6.0, ((0, 64), (1, 8)))
    out_weight = noise(splits[5], (HEADS * HEAD, D), (HEADS * HEAD) ** -0.5, 0.0625, ((0, 8), (1, 32)))
    decode_queries = draw_decode_queries(jax.random.fold_in(splits[14], 71), 0)
    decode_keys = draw_decode_keys(jax.random.fold_in(splits[14], 71), 0)
    decode_values = noise(splits[8], (ROWS, CTX_MAX, KV_HEADS * HEAD), 1.0, 6.0, ((0, 2), (1, 32), (2, 8)))
    new_keys = draw_new_keys(jax.random.fold_in(splits[14], 71), 0)
    new_values = noise(splits[10], (STEPS, ROWS, KV_HEADS * HEAD), 1.0, 6.0, ((1, 2), (2, 8)))
    request_lengths = set_ends(jax.random.randint(splits[11], (REQUESTS,), 1, CTX_MAX + 1), jax.random.fold_in(splits[11], 1), 1, CTX_MAX).astype(jnp.int32)
    row_requests = set_ends(jax.random.randint(splits[12], (ROWS,), 0, REQUESTS), jax.random.fold_in(splits[12], 1), 0, REQUESTS - 1).astype(jnp.int32)
    block_table_keys = jax.random.split(jax.random.fold_in(splits[13], 1), NBLOCKS // NBLOCKS)
    block_table_turns = jax.random.permutation(jax.random.fold_in(splits[13], 3), NBLOCKS // NBLOCKS)
    block_table = jax.vmap(lambda own, number: deal_out(jax.random.fold_in(splits[13], 2), own, number, NBLOCKS, OWNERS, 1, MOST, 2))(block_table_keys, block_table_turns).reshape((NBLOCKS, 1))
    return dict(prefill_queries=prefill_queries, cached_keys=cached_keys, cached_values=cached_values, span_keys=span_keys, span_values=span_values, out_weight=out_weight, decode_queries=decode_queries, decode_keys=decode_keys, decode_values=decode_values, new_keys=new_keys, new_values=new_values, request_lengths=request_lengths, row_requests=row_requests, block_table=block_table)


masked_score = -1.0e30


def reference(prefill_queries, cached_keys, cached_values, span_keys, span_values, out_weight, decode_queries, decode_keys, decode_values, new_keys, new_values, request_lengths, row_requests, block_table):
    score_scale = HEAD ** -0.5
    group_size = HEADS // KV_HEADS
    key_rows = jnp.concatenate([cached_keys, span_keys], axis=0).reshape(CONTEXT + SPAN, KV_HEADS, HEAD)
    value_rows = jnp.concatenate([cached_values, span_values], axis=0).reshape(CONTEXT + SPAN, KV_HEADS, HEAD)
    query_index = jnp.arange(SPAN, dtype=jnp.int32)
    key_index = jnp.arange(CONTEXT + SPAN, dtype=jnp.int32) - CONTEXT
    visible = key_index[None, :] <= query_index[:, None]
    queries = prefill_queries.reshape(SPAN, HEADS, HEAD).transpose(1, 0, 2)

    def one_head(inputs):
        query_rows, head_number = inputs
        keys_one = lax.dynamic_index_in_dim(key_rows, head_number // group_size, 1, keepdims=False)
        values_one = lax.dynamic_index_in_dim(value_rows, head_number // group_size, 1, keepdims=False)
        scores = jnp.einsum("qd,kd->qk", query_rows, keys_one, preferred_element_type=jnp.float32) * score_scale
        scores = jnp.where(visible, scores, masked_score)
        row_peak = jnp.max(scores, axis=1)
        weights = jnp.where(visible, jnp.exp(scores - row_peak[:, None]), 0.0)
        totals = jnp.sum(weights, axis=1)
        weighted = jnp.dot(weights.astype(jnp.bfloat16), values_one, preferred_element_type=jnp.float32)
        return (weighted / totals[:, None]).astype(jnp.bfloat16)

    attention = lax.map(one_head, (queries, jnp.arange(HEADS, dtype=jnp.int32)))
    attention = attention.transpose(1, 0, 2).reshape(SPAN, HEADS * HEAD)
    prefill_out = jnp.dot(attention, out_weight, preferred_element_type=jnp.float32).astype(jnp.bfloat16)

    dec_queries = decode_queries.astype(jnp.float32).reshape(STEPS, ROWS, KV_HEADS, group_size, HEAD)
    dec_keys = decode_keys.astype(jnp.float32).reshape(ROWS, CTX_MAX, KV_HEADS, HEAD)
    dec_values = decode_values.astype(jnp.float32).reshape(ROWS, CTX_MAX, KV_HEADS, HEAD)
    step_keys = new_keys.astype(jnp.float32).reshape(STEPS, ROWS, KV_HEADS, HEAD)
    step_values = new_values.astype(jnp.float32).reshape(STEPS, ROWS, KV_HEADS, HEAD)
    row_length = request_lengths[row_requests]
    live = jnp.arange(CTX_MAX, dtype=jnp.int32)[None, :] < row_length[:, None]
    causal = jnp.arange(STEPS, dtype=jnp.int32)[None, :] <= jnp.arange(STEPS, dtype=jnp.int32)[:, None]

    def one_group(kv_number):
        query_part = lax.dynamic_index_in_dim(dec_queries, kv_number, 2, keepdims=False)
        keys_part = lax.dynamic_index_in_dim(dec_keys, kv_number, 2, keepdims=False)
        values_part = lax.dynamic_index_in_dim(dec_values, kv_number, 2, keepdims=False)
        step_key_part = lax.dynamic_index_in_dim(step_keys, kv_number, 2, keepdims=False)
        step_value_part = lax.dynamic_index_in_dim(step_values, kv_number, 2, keepdims=False)
        cache_scores = jnp.einsum("trgd,rsd->rgts", query_part, keys_part) * score_scale
        cache_scores = jnp.where(live[:, None, None, :], cache_scores, masked_score)
        step_scores = jnp.einsum("trgd,urd->rgtu", query_part, step_key_part) * score_scale
        step_scores = jnp.where(causal, step_scores, masked_score)
        peak = jnp.maximum(jnp.max(cache_scores, axis=3), jnp.max(step_scores, axis=3))
        cache_weights = jnp.where(live[:, None, None, :], jnp.exp(cache_scores - peak[..., None]), 0.0)
        step_weights = jnp.where(causal, jnp.exp(step_scores - peak[..., None]), 0.0)
        totals = jnp.sum(cache_weights, axis=3) + jnp.sum(step_weights, axis=3)
        weighted = jnp.einsum("rgts,rsd->rgtd", cache_weights.astype(jnp.bfloat16).astype(jnp.float32), values_part)
        weighted = weighted + jnp.einsum("rgtu,urd->rgtd", step_weights.astype(jnp.bfloat16).astype(jnp.float32), step_value_part)
        return (weighted / totals[..., None]).astype(jnp.bfloat16)

    decoded = lax.map(one_group, jnp.arange(KV_HEADS, dtype=jnp.int32))
    decoded = decoded.transpose(3, 1, 0, 2, 4).reshape(STEPS * ROWS, HEADS * HEAD)
    decode_out = jnp.dot(decoded, out_weight, preferred_element_type=jnp.float32).astype(jnp.bfloat16).reshape(STEPS, ROWS, D)

    targets = block_table[:, 0]
    block_order = jnp.arange(NBLOCKS, dtype=jnp.int32)
    earlier = (targets[None, :] == targets[:, None]) & (block_order[None, :] < block_order[:, None])
    block_rank = jnp.sum(earlier.astype(jnp.int32), axis=1)
    owner_ids = jnp.arange(OWNERS, dtype=jnp.int32)
    slot_ids = jnp.arange(MOST, dtype=jnp.int32)
    chosen = (targets[None, None, :] == owner_ids[:, None, None]) & (block_rank[None, None, :] == slot_ids[None, :, None])
    chosen = chosen.astype(jnp.float32).reshape(OWNERS * MOST, NBLOCKS)
    key_blocks = span_keys.astype(jnp.float32).reshape(NBLOCKS, BLOCK * KV_HEADS * HEAD)
    value_blocks = span_values.astype(jnp.float32).reshape(NBLOCKS, BLOCK * KV_HEADS * HEAD)
    landed_keys = jnp.dot(chosen, key_blocks).astype(jnp.bfloat16).reshape(OWNERS, MOST, BLOCK, KV_HEADS * HEAD)
    landed_values = jnp.dot(chosen, value_blocks).astype(jnp.bfloat16).reshape(OWNERS, MOST, BLOCK, KV_HEADS * HEAD)
    return (prefill_out, decode_out, landed_keys, landed_values)
```

```python
import functools
import math

import jax
import jax.numpy as jnp
from jax import lax
from jax.experimental import pallas as pl
from jax.experimental.pallas import tpu as pltpu
from jax.sharding import Mesh
from jax.sharding import PartitionSpec as P

HEADS = 64
KV_HEADS = 8
HEAD = 128
SPAN = 512
BLOCK = 4
STEPS = 4
SEQ = ("seq_0", "seq_1")
SEQ_GROUP = ("seq_0", "seq_1", "group")
SEQ_TENSOR = ("seq_0", "seq_1", "tensor")

PEERS = 32
LOCAL = 8
ROWS = 16
SLOTS = 256
CACHED = 1024
HALF = 256
KEYS = 2 * CACHED + 128
STAT = LOCAL * HEAD
DEC = STAT + HEAD
WIDE = DEC + 2 * HEAD
THIN = STAT + 2 * HEAD
DEC_LANE = 32

NEG = -1e30
LOG2 = HEAD**-0.5 * math.log2(math.e)
bf16 = jnp.bfloat16
f32 = jnp.float32


def log_total(peak, total):
    safe = jnp.where(total > 0.0, total, 1.0)
    return jnp.where(total > 0.0, peak * LOG2 + jnp.log2(safe), NEG)


def terms(x):
    first = x.astype(bf16).astype(f32)
    rest = x - first
    second = rest.astype(bf16).astype(f32)
    return (first, second, rest - second)


def dot_t(a, b):
    return lax.dot_general(a, b, (((1,), (1,)), ((), ())), preferred_element_type=f32)


def dot(a, b):
    return lax.dot_general(a, b, (((1,), (0,)), ((), ())), preferred_element_type=f32)


def decode_kernel(place, lengths, requests, q_ref, k_ref, v_ref, nk_ref, nv_ref, out_ref, qs, os, ls, nks, nvs):
    lines = LOCAL * STEPS
    for h in range(LOCAL):
        for t in range(STEPS):
            at = (h * STEPS + t) * ROWS
            qs[at : at + ROWS, :] = q_ref[t, :, h * HEAD : (h + 1) * HEAD].astype(f32)
    for u in range(STEPS):
        nks[u * ROWS : (u + 1) * ROWS, :] = nk_ref[u].astype(f32)
        nvs[u * ROWS : (u + 1) * ROWS, :] = nv_ref[u].astype(f32)
    nks[STEPS * ROWS :, :] = jnp.zeros((STEPS * ROWS, HEAD), f32)
    nvs[STEPS * ROWS :, :] = jnp.zeros((STEPS * ROWS, HEAD), f32)
    seq = place[0]
    position = seq * SLOTS + lax.broadcasted_iota(jnp.int32, (lines, SLOTS), 1)
    step = lax.broadcasted_iota(jnp.int32, (lines, 8), 1)
    line_step = lax.broadcasted_iota(jnp.int32, (lines, 8), 0) % STEPS
    step_seen = (step <= line_step) & (seq == 0)
    for r in range(ROWS):
        length = lengths[requests[r]]
        q = qs[pl.ds(r, lines, stride=ROWS), :].astype(bf16)
        nk = nks[pl.ds(r, 8, stride=ROWS), :].astype(bf16)
        nv = nvs[pl.ds(r, 8, stride=ROWS), :].astype(bf16)
        s = dot_t(q, k_ref[r])
        s2 = dot_t(q, nk)
        seen = position < length
        s = jnp.where(seen, s, NEG)
        s2 = jnp.where(step_seen, s2, NEG)
        peak = jnp.maximum(jnp.max(s, axis=1, keepdims=True), jnp.max(s2, axis=1, keepdims=True))
        p = jnp.where(seen, jnp.exp2((s - peak) * LOG2), 0.0)
        p2 = jnp.where(step_seen, jnp.exp2((s2 - peak) * LOG2), 0.0)
        total = jnp.sum(p, axis=1, keepdims=True) + jnp.sum(p2, axis=1, keepdims=True)
        o = dot(p.astype(bf16), v_ref[r]) + dot(p2.astype(bf16), nv)
        o = o / jnp.where(total > 0.0, total, 1.0)
        os[pl.ds(r, lines, stride=ROWS), :] = o
        ls[pl.ds(r, lines, stride=ROWS), :] = jnp.broadcast_to(log_total(peak, total), (lines, HEAD))
    o = os[...].reshape(PEERS, 2, 8, HEAD)
    logs = ls[...].reshape(PEERS, 2, 8, HEAD)
    lane = lax.broadcasted_iota(jnp.int32, (PEERS, 8, HEAD), 2)
    stat = jnp.zeros((PEERS, 8, HEAD), f32)
    for b in range(2):
        out_ref[:, :, b * HEAD : (b + 1) * HEAD] = o[:, b].astype(bf16)
        for i, term in enumerate(terms(logs[:, b])):
            stat = jnp.where(lane == DEC_LANE + 3 * b + i, term, stat)
    out_ref[:, :, 2 * HEAD :] = stat.astype(bf16)


def prefill_kernel(place, q_ref, k_ref, v_ref, sk_ref, sv_ref, other_ref, dec_ref, out_ref, keys, values, stat):
    h = pl.program_id(0)
    seq, group = place[0], place[1]

    @pl.when(h == 0)
    def _():
        own_k, own_v = sk_ref[...].astype(f32), sv_ref[...].astype(f32)
        far = other_ref[2 * CACHED :, :].astype(f32)
        far_k, far_v = far[:8], far[8:]
        first = jnp.full((8, HEAD), group, jnp.int32) == 0
        near = jnp.concatenate([jnp.where(first, own_k, far_k), jnp.where(first, far_k, own_k)], axis=0)
        near_v = jnp.concatenate([jnp.where(first, own_v, far_v), jnp.where(first, far_v, own_v)], axis=0)
        keys[0:CACHED, :] = k_ref[...]
        keys[CACHED : 2 * CACHED, :] = other_ref[0:CACHED, :]
        values[0:CACHED, :] = v_ref[...]
        values[CACHED : 2 * CACHED, :] = other_ref[CACHED : 2 * CACHED, :]
        keys[2 * CACHED :, :] = jnp.zeros((HEAD, HEAD), bf16)
        values[2 * CACHED :, :] = jnp.zeros((HEAD, HEAD), bf16)
        keys[2 * CACHED : 2 * CACHED + 16, :] = near.astype(bf16)
        values[2 * CACHED : 2 * CACHED + 16, :] = near_v.astype(bf16)
        out_ref[:, :, DEC:] = dec_ref[:, :, 0 : 2 * HEAD]
        stat[...] = dec_ref[:, :, 2 * HEAD :].astype(f32)

    lane = lax.broadcasted_iota(jnp.int32, (PEERS // 2, 8, HEAD), 2)
    part = HALF // 2
    for b in range(2):
        rows = slice(b * part, (b + 1) * part)
        blocks = slice(b * PEERS // 2, (b + 1) * PEERS // 2)
        q = q_ref[rows, :]
        s = dot_t(q, keys[0 : 2 * CACHED, :])
        s2 = dot_t(q, keys[2 * CACHED :, :])
        index = lax.broadcasted_iota(jnp.int32, (part, HEAD), 1)
        query = group * HALF + b * part + lax.broadcasted_iota(jnp.int32, (part, HEAD), 0)
        seen = (index < 16) & (seq * 16 + index <= query)
        s2 = jnp.where(seen, s2, NEG)
        peak = jnp.maximum(jnp.max(s, axis=1, keepdims=True), jnp.max(s2, axis=1, keepdims=True))
        p = jnp.exp2((s - peak) * LOG2)
        p2 = jnp.where(seen, jnp.exp2((s2 - peak) * LOG2), 0.0)
        total = jnp.sum(p, axis=1, keepdims=True) + jnp.sum(p2, axis=1, keepdims=True)
        o = dot(p.astype(bf16), values[0 : 2 * CACHED, :]) + dot(p2.astype(bf16), values[2 * CACHED :, :])
        o = (o / total).reshape(PEERS // 2, 8, HEAD)
        out_ref[blocks, :, pl.ds(pl.multiple_of(h * HEAD, HEAD), HEAD)] = o.astype(bf16)
        logs = jnp.broadcast_to(log_total(peak, total), (part, HEAD)).reshape(PEERS // 2, 8, HEAD)
        now = stat[blocks]
        for i, term in enumerate(terms(logs)):
            now = jnp.where(lane == 3 * h + i, term, now)
        stat[blocks] = now

    @pl.when(h == LOCAL - 1)
    def _():
        out_ref[:, :, STAT:DEC] = stat[...].astype(bf16)


def combine_kernel(in_ref, out_ref):
    t = in_ref[:, :, STAT:DEC].astype(f32).reshape(PEERS * 8, HEAD)
    logs = t + pltpu.roll(t, HEAD - 1, 1) + pltpu.roll(t, HEAD - 2, 1)
    logs = logs.reshape(PEERS, 8, HEAD)
    share = jnp.exp2(logs - jnp.max(logs, axis=0)[None])
    share = share / jnp.sum(share, axis=0)[None]
    for j in range(LOCAL + 2):
        lane = 3 * j if j < LOCAL else DEC_LANE + 3 * (j - LOCAL)
        at = j * HEAD if j < LOCAL else DEC + (j - LOCAL) * HEAD
        x = in_ref[:, :, at : at + HEAD].astype(f32)
        total = jnp.sum(x * share[:, :, lane : lane + 1], axis=0)
        out_ref[:, :, j * HEAD : (j + 1) * HEAD] = jnp.broadcast_to(total[None], (PEERS, 8, HEAD)).astype(bf16)


def project_kernel(in_ref, w_ref, out_ref, rows):
    rows[0:HALF, :] = in_ref[:, :, 0:STAT].astype(f32).reshape(HALF, STAT)
    for h in range(LOCAL):
        for t in range(STEPS):
            for b in range(2):
                at = HALF + t * ROWS + b * 8
                x = in_ref[h * STEPS + t, :, STAT + b * HEAD : STAT + (b + 1) * HEAD]
                rows[at : at + 8, h * HEAD : (h + 1) * HEAD] = x.astype(f32)
    y = dot(rows[...].astype(bf16), w_ref[...])
    y = jnp.concatenate([y, jnp.zeros((HEAD // 2, y.shape[1]), f32)], axis=0)
    y = y.T
    out_ref[...] = y.reshape(8, 32, 3 * HEAD)


def last_kernel(in_ref, prefill_ref, decode_ref):
    y = jnp.sum(in_ref[...], axis=0)
    prefill_ref[...] = y[:, 0:HALF].astype(bf16)
    decode_ref[...] = y[:, HALF : HALF + HEAD].T[: STEPS * ROWS].reshape(STEPS, ROWS, 32).astype(bf16)


def landing_kernel(place, row_ref, in_ref, keys_ref, values_ref):
    owner = place[0] * 2 + place[1]
    blocks = SPAN // BLOCK
    row = row_ref[...]
    column = jnp.broadcast_to(row.astype(f32), (blocks, blocks)).T.astype(jnp.int32)
    earlier = lax.broadcasted_iota(jnp.int32, (blocks, blocks), 0) < lax.broadcasted_iota(
        jnp.int32, (blocks, blocks), 1
    )
    same = (column == row) & earlier
    rank = jnp.sum(jnp.where(same, 1.0, 0.0), axis=0, keepdims=True)
    code = jnp.broadcast_to(jnp.where(row == owner, rank, -1.0), (16, blocks)).astype(bf16)
    spread = lax.broadcasted_iota(jnp.int32, (blocks, SPAN), 1) // BLOCK
    spread = spread == lax.broadcasted_iota(jnp.int32, (blocks, SPAN), 0)
    code = dot(code, jnp.where(spread, 1.0, 0.0).astype(bf16))
    line = lax.broadcasted_iota(jnp.int32, (16, SPAN), 0)
    token = lax.broadcasted_iota(jnp.int32, (16, SPAN), 1) % BLOCK
    chosen = (code == (line // BLOCK).astype(f32)) & (token == line % BLOCK)
    x = in_ref[...].reshape(SPAN, 2 * HEAD)
    y = dot(jnp.where(chosen, 1.0, 0.0).astype(bf16), x)
    keys_ref[...] = y[:, :HEAD].astype(bf16)
    values_ref[...] = y[:, HEAD:].astype(bf16)


def cost(flops, moved, exps=0):
    return pl.CostEstimate(flops=flops, bytes_accessed=moved, transcendentals=exps)


SMEM = pl.BlockSpec(memory_space=pltpu.SMEM)
VMEM = pl.BlockSpec(memory_space=pltpu.VMEM)


def swap(x, axis):
    return lax.all_to_all(x, axis, 0, 0, tiled=True)


def body(
    prefill_queries,
    cached_keys,
    cached_values,
    span_keys,
    span_values,
    out_weight,
    decode_queries,
    decode_keys,
    decode_values,
    new_keys,
    new_values,
    request_lengths,
    row_requests,
    block_table,
):
    seq = lax.axis_index(SEQ)
    group = lax.axis_index("group")
    place = jnp.stack([seq, group]).astype(jnp.int32)
    blocks = jnp.concatenate([span_keys, span_values], axis=1)
    landed = swap(jnp.broadcast_to(blocks[None], (2 * PEERS, *blocks.shape)), SEQ_GROUP)
    mine = jnp.concatenate([cached_keys, cached_values, span_keys, span_values], axis=0)
    other = lax.ppermute(mine, "group", [(0, 1), (1, 0)])

    lines = LOCAL * STEPS * ROWS
    decoded = pl.pallas_call(
        decode_kernel,
        name="decode",
        out_shape=jax.ShapeDtypeStruct((PEERS, 8, 3 * HEAD), bf16),
        in_specs=[SMEM] * 3 + [VMEM] * 5,
        out_specs=VMEM,
        scratch_shapes=[pltpu.VMEM((lines, HEAD), f32)] * 3 + [pltpu.VMEM((2 * STEPS * ROWS, HEAD), f32)] * 2,
        cost_estimate=cost(2 * 2 * 512 * SLOTS * HEAD * 8, 3 << 20, 512 * SLOTS),
    )(place, request_lengths, row_requests, decode_queries, decode_keys, decode_values, new_keys, new_values)

    whole2 = lambda h, place: (0, 0)
    whole3 = lambda h, place: (0, 0, 0)
    packed = pl.pallas_call(
        prefill_kernel,
        name="prefill",
        out_shape=jax.ShapeDtypeStruct((PEERS, 8, WIDE), bf16),
        grid_spec=pltpu.PrefetchScalarGridSpec(
            num_scalar_prefetch=1,
            grid=(LOCAL,),
            in_specs=[
                pl.BlockSpec((HALF, HEAD), lambda h, place: (place[1], h)),
                pl.BlockSpec((CACHED, HEAD), whole2),
                pl.BlockSpec((CACHED, HEAD), whole2),
                pl.BlockSpec((8, HEAD), whole2),
                pl.BlockSpec((8, HEAD), whole2),
                pl.BlockSpec((2 * CACHED + 16, HEAD), whole2),
                pl.BlockSpec((PEERS, 8, 3 * HEAD), whole3),
            ],
            out_specs=pl.BlockSpec((PEERS, 8, WIDE), whole3),
            scratch_shapes=[
                pltpu.VMEM((KEYS, HEAD), bf16),
                pltpu.VMEM((KEYS, HEAD), bf16),
                pltpu.VMEM((PEERS, 8, HEAD), f32),
            ],
        ),
        compiler_params=pltpu.CompilerParams(dimension_semantics=("arbitrary",)),
        cost_estimate=cost(4 * HALF * LOCAL * KEYS * HEAD, 4 << 20, HALF * LOCAL * KEYS),
    )(place, prefill_queries, cached_keys, cached_values, span_keys, span_values, other, decoded)

    arrived = swap(packed, SEQ)
    arrived, landed = lax.optimization_barrier((arrived, landed))
    attention = pl.pallas_call(
        combine_kernel,
        name="combine",
        out_shape=jax.ShapeDtypeStruct((PEERS, 8, THIN), bf16),
        in_specs=[VMEM],
        out_specs=VMEM,
        cost_estimate=cost(1 << 20, 2 << 20),
    )(arrived)
    attention = swap(attention, SEQ)
    columns = out_weight.shape[1]
    partial = pl.pallas_call(
        project_kernel,
        name="project",
        out_shape=jax.ShapeDtypeStruct((8, columns // 8, 3 * HEAD), f32),
        in_specs=[VMEM] * 2,
        out_specs=VMEM,
        scratch_shapes=[pltpu.VMEM((HALF + STEPS * ROWS, STAT), f32)],
        cost_estimate=cost(2 * 320 * STAT * columns, 2 << 20),
    )(attention, out_weight)
    partial = swap(partial, "tensor")
    prefill_out, decode_out = pl.pallas_call(
        last_kernel,
        name="last",
        out_shape=(
            jax.ShapeDtypeStruct((columns // 8, HALF), bf16),
            jax.ShapeDtypeStruct((STEPS, ROWS, columns // 8), bf16),
        ),
        in_specs=[VMEM],
        out_specs=(VMEM, VMEM),
        cost_estimate=cost(1 << 18, 1 << 19),
    )(partial)
    landed_keys, landed_values = pl.pallas_call(
        landing_kernel,
        name="landing",
        out_shape=(jax.ShapeDtypeStruct((16, HEAD), bf16), jax.ShapeDtypeStruct((16, HEAD), bf16)),
        in_specs=[SMEM] + [VMEM] * 2,
        out_specs=(VMEM, VMEM),
        cost_estimate=cost(1 << 22, 1 << 19),
    )(place, block_table.reshape(1, -1), landed)
    shape = (1, 4, BLOCK, HEAD)
    return (prefill_out.T, decode_out, landed_keys.reshape(shape), landed_values.reshape(shape))


def solution(mesh):
    torus = Mesh(
        mesh.devices.reshape(4, 8, mesh.shape["tensor"], mesh.shape["group"]),
        ("seq_0", "seq_1", "tensor", "group"),
    )
    in_specs = (
        P(None, "tensor"),
        P(SEQ_GROUP, "tensor"),
        P(SEQ_GROUP, "tensor"),
        P(SEQ_GROUP, "tensor"),
        P(SEQ_GROUP, "tensor"),
        P("tensor", SEQ),
        P(None, "group", "tensor"),
        P("group", SEQ, "tensor"),
        P("group", SEQ, "tensor"),
        P(None, "group", "tensor"),
        P(None, "group", "tensor"),
        P(),
        P("group"),
        P(),
    )
    out_specs = (
        P("group", SEQ_TENSOR),
        P(None, "group", SEQ_TENSOR),
        P(SEQ_GROUP, None, None, "tensor"),
        P(SEQ_GROUP, None, None, "tensor"),
    )
    return jax.shard_map(body, mesh=torus, in_specs=in_specs, out_specs=out_specs, check_vma=False)
```

```python
import functools
import math

import jax
import jax.numpy as jnp
from jax import lax
from jax.experimental import pallas as pl
from jax.experimental.pallas import tpu as pltpu
from jax.sharding import Mesh
from jax.sharding import PartitionSpec as P

HEADS = 64
KV_HEADS = 8
HEAD = 128
SPAN = 512
BLOCK = 4
STEPS = 4
SEQ = ("seq_0", "seq_1")
SEQ_GROUP = ("seq_0", "seq_1", "group")
SEQ_TENSOR = ("seq_0", "seq_1", "tensor")

PEERS = 32
LOCAL = 8
ROWS = 16
SLOTS = 256
CACHED = 1024
HALF = 256
KEYS = 2 * CACHED + 128
STAT = LOCAL * HEAD
DEC = STAT + HEAD
NEW = DEC + 2 * HEAD
WIDE = NEW + 2 * HEAD
THIN = STAT + 2 * HEAD
DEC_LANE = 32

NEG = -1e30
LOG2 = HEAD**-0.5 * math.log2(math.e)
bf16 = jnp.bfloat16
f32 = jnp.float32


def log_total(peak, total):
    safe = jnp.where(total > 0.0, total, 1.0)
    return jnp.where(total > 0.0, peak * LOG2 + jnp.log2(safe), NEG)


def terms(x):
    first = x.astype(bf16).astype(f32)
    rest = x - first
    second = rest.astype(bf16).astype(f32)
    return (first, second, rest - second)


def dot_t(a, b):
    return lax.dot_general(a, b, (((1,), (1,)), ((), ())), preferred_element_type=f32)


def dot(a, b):
    return lax.dot_general(a, b, (((1,), (0,)), ((), ())), preferred_element_type=f32)


def decode_kernel(lengths, requests, q_ref, k_ref, v_ref, nk_ref, nv_ref, out_ref, qs, os, ls, nks, nvs):
    lines = LOCAL * STEPS
    for h in range(LOCAL):
        for t in range(STEPS):
            at = (h * STEPS + t) * ROWS
            qs[at : at + ROWS, :] = q_ref[t, :, h * HEAD : (h + 1) * HEAD].astype(f32)
    for u in range(STEPS):
        nks[u * ROWS : (u + 1) * ROWS, :] = nk_ref[u].astype(f32)
        nvs[u * ROWS : (u + 1) * ROWS, :] = nv_ref[u].astype(f32)
    nks[STEPS * ROWS :, :] = jnp.zeros((STEPS * ROWS, HEAD), f32)
    nvs[STEPS * ROWS :, :] = jnp.zeros((STEPS * ROWS, HEAD), f32)
    seq = lax.axis_index(SEQ)
    position = seq * SLOTS + lax.broadcasted_iota(jnp.int32, (lines, SLOTS), 1)
    step = lax.broadcasted_iota(jnp.int32, (ROWS * lines, 8), 1)
    line_step = lax.broadcasted_iota(jnp.int32, (ROWS * lines, 8), 0) % STEPS
    step_seen = (step <= line_step) & (seq == 0)
    scores, step_scores, step_values = [], [], []
    for r in range(ROWS):
        q = qs[pl.ds(r, lines, stride=ROWS), :].astype(bf16)
        nk = nks[pl.ds(r, 8, stride=ROWS), :].astype(bf16)
        step_values.append(nvs[pl.ds(r, 8, stride=ROWS), :].astype(bf16))
        scores.append(jnp.where(position < lengths[requests[r]], dot_t(q, k_ref[r]), NEG))
        step_scores.append(dot_t(q, nk))
    s = jnp.concatenate(scores, axis=0)
    s2 = jnp.where(step_seen, jnp.concatenate(step_scores, axis=0), NEG)
    peak = jnp.maximum(jnp.max(s, axis=1, keepdims=True), jnp.max(s2, axis=1, keepdims=True))
    p = jnp.where(s > 0.5 * NEG, jnp.exp2((s - peak) * LOG2), 0.0)
    p2 = jnp.where(step_seen, jnp.exp2((s2 - peak) * LOG2), 0.0)
    total = jnp.sum(p, axis=1, keepdims=True) + jnp.sum(p2, axis=1, keepdims=True)
    p, p2 = p.astype(bf16), p2.astype(bf16)
    inverse = 1.0 / jnp.where(total > 0.0, total, 1.0)
    logs = log_total(peak, total)
    for r in range(ROWS):
        at = slice(r * lines, (r + 1) * lines)
        o = dot(p[at], v_ref[r]) + dot(p2[at], step_values[r])
        os[pl.ds(r, lines, stride=ROWS), :] = o * inverse[at]
        ls[pl.ds(r, lines, stride=ROWS), :] = jnp.broadcast_to(logs[at], (lines, HEAD))
    o = os[...].reshape(PEERS, 2, 8, HEAD)
    logs = ls[...].reshape(PEERS, 2, 8, HEAD)
    lane = lax.broadcasted_iota(jnp.int32, (PEERS, 8, HEAD), 2)
    stat = jnp.zeros((PEERS, 8, HEAD), f32)
    for b in range(2):
        out_ref[:, :, b * HEAD : (b + 1) * HEAD] = o[:, b].astype(bf16)
        for i, term in enumerate(terms(logs[:, b])):
            stat = jnp.where(lane == DEC_LANE + 3 * b + i, term, stat)
    out_ref[:, :, 2 * HEAD :] = stat.astype(bf16)


def prefill_kernel(q_ref, k_ref, v_ref, sk_ref, sv_ref, other_ref, dec_ref, out_ref, keys, values):
    seq, group = lax.axis_index(SEQ), lax.axis_index("group")
    own_k, own_v = sk_ref[...].astype(f32), sv_ref[...].astype(f32)
    far = other_ref[2 * CACHED :, :].astype(f32)
    far_k, far_v = far[:8], far[8:]
    first = jnp.full((8, HEAD), group, jnp.int32) == 0
    near_k = jnp.concatenate([jnp.where(first, own_k, far_k), jnp.where(first, far_k, own_k)], axis=0)
    near_v = jnp.concatenate([jnp.where(first, own_v, far_v), jnp.where(first, far_v, own_v)], axis=0)
    keys[0:CACHED, :] = k_ref[...]
    keys[CACHED : 2 * CACHED, :] = other_ref[0:CACHED, :]
    values[0:CACHED, :] = v_ref[...]
    values[CACHED : 2 * CACHED, :] = other_ref[CACHED : 2 * CACHED, :]
    keys[2 * CACHED :, :] = jnp.zeros((HEAD, HEAD), bf16)
    values[2 * CACHED :, :] = jnp.zeros((HEAD, HEAD), bf16)
    keys[2 * CACHED : 2 * CACHED + 16, :] = near_k.astype(bf16)
    values[2 * CACHED : 2 * CACHED + 16, :] = near_v.astype(bf16)
    out_ref[:, :, DEC:NEW] = dec_ref[:, :, 0 : 2 * HEAD]
    out_ref[:, :, NEW : NEW + HEAD] = jnp.broadcast_to(own_k[None], (PEERS, 8, HEAD)).astype(bf16)
    out_ref[:, :, NEW + HEAD :] = jnp.broadcast_to(own_v[None], (PEERS, 8, HEAD)).astype(bf16)

    lane = lax.broadcasted_iota(jnp.int32, (PEERS, 8, HEAD), 2)
    index = lax.broadcasted_iota(jnp.int32, (HALF, HEAD), 1)
    query = group * HALF + lax.broadcasted_iota(jnp.int32, (HALF, HEAD), 0)
    seen = (index < 16) & (seq * 16 + index <= query)
    mine = pl.ds(pl.multiple_of(group * HALF, HALF), HALF)

    def scores(h):
        s = dot_t(q_ref[mine, h * HEAD : (h + 1) * HEAD], keys[...])
        return jnp.concatenate([s[:, : 2 * CACHED], jnp.where(seen, s[:, 2 * CACHED :], NEG)], axis=1)

    upcoming = scores(0)
    stat = dec_ref[:, :, 2 * HEAD :].astype(f32)
    for h in range(LOCAL):
        s = upcoming
        if h + 1 < LOCAL:
            upcoming = scores(h + 1)
        peak = jnp.max(s, axis=1, keepdims=True)
        edge = s[:, 2 * CACHED :]
        p = jnp.exp2((s[:, : 2 * CACHED] - peak) * LOG2)
        p = jnp.concatenate([p, jnp.where(seen, jnp.exp2((edge - peak) * LOG2), 0.0)], axis=1)
        total = jnp.sum(p, axis=1, keepdims=True)
        o = dot(p.astype(bf16), values[...])
        o = (o / total).reshape(PEERS, 8, HEAD)
        out_ref[:, :, h * HEAD : (h + 1) * HEAD] = o.astype(bf16)
        logs = jnp.broadcast_to(log_total(peak, total), (HALF, HEAD)).reshape(PEERS, 8, HEAD)
        for i, term in enumerate(terms(logs)):
            stat = jnp.where(lane == 3 * h + i, term, stat)
    out_ref[:, :, STAT:DEC] = stat.astype(bf16)


def combine_kernel(in_ref, out_ref, new_ref):
    new_ref[...] = in_ref[:, :, NEW:]
    t = in_ref[:, :, STAT:DEC].astype(f32).reshape(PEERS * 8, HEAD)
    logs = t + pltpu.roll(t, HEAD - 1, 1) + pltpu.roll(t, HEAD - 2, 1)
    logs = logs.reshape(PEERS, 8, HEAD)
    share = jnp.exp2(logs - jnp.max(logs, axis=0)[None])
    share = share / jnp.sum(share, axis=0)[None]
    for j in range(LOCAL + 2):
        lane = 3 * j if j < LOCAL else DEC_LANE + 3 * (j - LOCAL)
        at = j * HEAD if j < LOCAL else DEC + (j - LOCAL) * HEAD
        x = in_ref[:, :, at : at + HEAD].astype(f32)
        total = jnp.sum(x * share[:, :, lane : lane + 1], axis=0)
        out_ref[:, :, j * HEAD : (j + 1) * HEAD] = jnp.broadcast_to(total[None], (PEERS, 8, HEAD)).astype(bf16)


def project_kernel(in_ref, w_ref, out_ref, rows):
    rows[0:HALF, :] = in_ref[:, :, 0:STAT].astype(f32).reshape(HALF, STAT)
    for h in range(LOCAL):
        for t in range(STEPS):
            for b in range(2):
                at = HALF + t * ROWS + b * 8
                x = in_ref[h * STEPS + t, :, STAT + b * HEAD : STAT + (b + 1) * HEAD]
                rows[at : at + 8, h * HEAD : (h + 1) * HEAD] = x.astype(f32)
    y = dot(rows[...].astype(bf16), w_ref[...])
    y = jnp.concatenate([y, jnp.zeros((HEAD // 2, y.shape[1]), f32)], axis=0)
    y = y.T
    out_ref[...] = y.reshape(8, 32, 3 * HEAD).astype(bf16)


def last_kernel(in_ref, prefill_ref, decode_ref):
    y = jnp.sum(in_ref[...].astype(f32), axis=0)
    prefill_ref[...] = y[:, 0:HALF].astype(bf16)
    decode_ref[...] = y[:, HALF : HALF + HEAD].T[: STEPS * ROWS].reshape(STEPS, ROWS, 32).astype(bf16)


def landing_kernel(row_ref, own_ref, far_ref, keys_ref, values_ref):
    group = lax.axis_index("group")
    owner = lax.axis_index(SEQ) * 2 + group
    blocks, tokens = SPAN // BLOCK, SPAN // 2
    row = row_ref[...]
    column = jnp.broadcast_to(row.astype(f32), (blocks, blocks)).T.astype(jnp.int32)
    earlier = lax.broadcasted_iota(jnp.int32, (blocks, blocks), 0) < lax.broadcasted_iota(
        jnp.int32, (blocks, blocks), 1
    )
    same = (column == row) & earlier
    rank = jnp.sum(jnp.where(same, 1.0, 0.0), axis=0, keepdims=True)
    code = jnp.broadcast_to(jnp.where(row == owner, rank, -1.0), (16, blocks)).astype(bf16)
    token = lax.broadcasted_iota(jnp.int32, (blocks, tokens), 1)
    block = lax.broadcasted_iota(jnp.int32, (blocks, tokens), 0)
    line = lax.broadcasted_iota(jnp.int32, (16, tokens), 0)
    place_in = lax.broadcasted_iota(jnp.int32, (16, tokens), 1) % BLOCK

    def picked(side, ref):
        spread = (token // 8) * 4 + side * 2 + (token % 8) // BLOCK == block
        codes = dot(code, jnp.where(spread, 1.0, 0.0).astype(bf16))
        chosen = (codes == (line // BLOCK).astype(f32)) & (place_in == line % BLOCK)
        x = ref[...].astype(f32).reshape(tokens, 2 * HEAD).astype(bf16)
        return dot(jnp.where(chosen, 1.0, 0.0).astype(bf16), x)

    y = picked(group, own_ref) + picked(1 - group, far_ref)
    keys_ref[...] = y[:, :HEAD].astype(bf16)
    values_ref[...] = y[:, HEAD:].astype(bf16)


def cost(flops, moved, exps=0):
    return pl.CostEstimate(flops=flops, bytes_accessed=moved, transcendentals=exps)


SMEM = pl.BlockSpec(memory_space=pltpu.SMEM)
VMEM = pl.BlockSpec(memory_space=pltpu.VMEM)


def near(x):
    return pltpu.with_memory_space_constraint(x, pltpu.VMEM)


def swap(x, axis):
    return lax.all_to_all(x, axis, 0, 0, tiled=True)


def body(
    prefill_queries,
    cached_keys,
    cached_values,
    span_keys,
    span_values,
    out_weight,
    decode_queries,
    decode_keys,
    decode_values,
    new_keys,
    new_values,
    request_lengths,
    row_requests,
    block_table,
):
    mine = jnp.concatenate([cached_keys, cached_values, span_keys, span_values], axis=0)
    other = lax.ppermute(mine, "group", [(0, 1), (1, 0)])

    lines = LOCAL * STEPS * ROWS
    decoded = pl.pallas_call(
        decode_kernel,
        name="decode",
        out_shape=jax.ShapeDtypeStruct((PEERS, 8, 3 * HEAD), bf16),
        in_specs=[SMEM] * 2 + [VMEM] * 5,
        out_specs=VMEM,
        scratch_shapes=[pltpu.VMEM((lines, HEAD), f32)] * 3 + [pltpu.VMEM((2 * STEPS * ROWS, HEAD), f32)] * 2,
        cost_estimate=cost(2 * 2 * 512 * SLOTS * HEAD * 8, 3 << 20, 512 * SLOTS),
    )(request_lengths, row_requests, decode_queries, decode_keys, decode_values, new_keys, new_values)

    packed = pl.pallas_call(
        prefill_kernel,
        name="prefill",
        out_shape=jax.ShapeDtypeStruct((PEERS, 8, WIDE), bf16),
        in_specs=[VMEM] * 7,
        out_specs=VMEM,
        scratch_shapes=[pltpu.VMEM((KEYS, HEAD), bf16)] * 2,
        cost_estimate=cost(4 * HALF * LOCAL * KEYS * HEAD, 4 << 20, HALF * LOCAL * KEYS),
    )(
        near(prefill_queries),
        near(cached_keys),
        near(cached_values),
        span_keys,
        span_values,
        near(other),
        decoded,
    )

    arrived = swap(packed, SEQ)
    attention, new_own = pl.pallas_call(
        combine_kernel,
        name="combine",
        out_shape=(
            jax.ShapeDtypeStruct((PEERS, 8, THIN), bf16),
            jax.ShapeDtypeStruct((PEERS, 8, 2 * HEAD), bf16),
        ),
        in_specs=[VMEM],
        out_specs=(VMEM, VMEM),
        cost_estimate=cost(1 << 20, 2 << 20),
    )(near(arrived))
    new_far = lax.ppermute(new_own, "group", [(0, 1), (1, 0)])
    attention = swap(attention, SEQ)
    landed_keys, landed_values = pl.pallas_call(
        landing_kernel,
        name="landing",
        out_shape=(jax.ShapeDtypeStruct((16, HEAD), bf16), jax.ShapeDtypeStruct((16, HEAD), bf16)),
        in_specs=[VMEM] * 3,
        out_specs=(VMEM, VMEM),
        cost_estimate=cost(1 << 22, 1 << 19),
    )(block_table.reshape(1, -1), near(new_own), near(new_far))
    attention, landed_keys, landed_values = lax.optimization_barrier((attention, landed_keys, landed_values))
    columns = out_weight.shape[1]
    partial = pl.pallas_call(
        project_kernel,
        name="project",
        out_shape=jax.ShapeDtypeStruct((8, columns // 8, 3 * HEAD), bf16),
        in_specs=[VMEM] * 2,
        out_specs=VMEM,
        scratch_shapes=[pltpu.VMEM((HALF + STEPS * ROWS, STAT), f32)],
        cost_estimate=cost(2 * 320 * STAT * columns, 2 << 20),
    )(near(attention), near(out_weight))
    partial = swap(partial, "tensor")
    prefill_out, decode_out = pl.pallas_call(
        last_kernel,
        name="last",
        out_shape=(
            jax.ShapeDtypeStruct((columns // 8, HALF), bf16),
            jax.ShapeDtypeStruct((STEPS, ROWS, columns // 8), bf16),
        ),
        in_specs=[VMEM],
        out_specs=(VMEM, VMEM),
        cost_estimate=cost(1 << 18, 1 << 19),
    )(near(partial))
    shape = (1, 4, BLOCK, HEAD)
    return (prefill_out.T, decode_out, landed_keys.reshape(shape), landed_values.reshape(shape))


def solution(mesh):
    torus = Mesh(
        mesh.devices.reshape(4, 8, mesh.shape["tensor"], mesh.shape["group"]),
        ("seq_0", "seq_1", "tensor", "group"),
    )
    in_specs = (
        P(None, "tensor"),
        P(SEQ_GROUP, "tensor"),
        P(SEQ_GROUP, "tensor"),
        P(SEQ_GROUP, "tensor"),
        P(SEQ_GROUP, "tensor"),
        P("tensor", SEQ),
        P(None, "group", "tensor"),
        P("group", SEQ, "tensor"),
        P("group", SEQ, "tensor"),
        P(None, "group", "tensor"),
        P(None, "group", "tensor"),
        P(),
        P("group"),
        P(),
    )
    out_specs = (
        P("group", SEQ_TENSOR),
        P(None, "group", SEQ_TENSOR),
        P(SEQ_GROUP, None, None, "tensor"),
        P(SEQ_GROUP, None, None, "tensor"),
    )
    return jax.shard_map(body, mesh=torus, in_specs=in_specs, out_specs=out_specs, check_vma=False)
```

```python
import functools
import math

import jax
import jax.numpy as jnp
from jax import lax
from jax.experimental import pallas as pl
from jax.experimental.pallas import tpu as pltpu
from jax.sharding import Mesh
from jax.sharding import PartitionSpec as P

HEADS = 64
KV_HEADS = 8
HEAD = 128
SPAN = 512
BLOCK = 4
STEPS = 4
SEQ = ("seq_0", "seq_1", "pair")
SEQ_GROUP = (*SEQ, "group")
SEQ_TENSOR = (*SEQ, "tensor")

PEERS = 32
MATES = PEERS // 2
LOCAL = 8
ROWS = 16
SLOTS = 256
CACHED = 1024
HALF = 256
KEYS = 2 * CACHED + 128
STAT = LOCAL * HEAD
DEC = STAT + HEAD
NEW = DEC + 2 * HEAD
WIDE = NEW + 2 * HEAD
THIN = STAT + 2 * HEAD
DEC_LANE = 32

NEG = -1e30
LOG2 = HEAD**-0.5 * math.log2(math.e)
bf16 = jnp.bfloat16
f32 = jnp.float32


def log_total(peak, total):
    safe = jnp.where(total > 0.0, total, 1.0)
    return jnp.where(total > 0.0, peak * LOG2 + jnp.log2(safe), NEG)


def terms(x):
    first = x.astype(bf16).astype(f32)
    rest = x - first
    second = rest.astype(bf16).astype(f32)
    return (first, second, rest - second)


def dot_t(a, b):
    return lax.dot_general(a, b, (((1,), (1,)), ((), ())), preferred_element_type=f32)


def dot(a, b):
    return lax.dot_general(a, b, (((1,), (0,)), ((), ())), preferred_element_type=f32)


def decode_kernel(lengths, requests, q_ref, k_ref, v_ref, nk_ref, nv_ref, out_ref, qs, os, ls, nks, nvs):
    lines = LOCAL * STEPS
    for h in range(LOCAL):
        for t in range(STEPS):
            at = (h * STEPS + t) * ROWS
            qs[at : at + ROWS, :] = q_ref[t, :, h * HEAD : (h + 1) * HEAD].astype(f32)
    for u in range(STEPS):
        nks[u * ROWS : (u + 1) * ROWS, :] = nk_ref[u].astype(f32)
        nvs[u * ROWS : (u + 1) * ROWS, :] = nv_ref[u].astype(f32)
    nks[STEPS * ROWS :, :] = jnp.zeros((STEPS * ROWS, HEAD), f32)
    nvs[STEPS * ROWS :, :] = jnp.zeros((STEPS * ROWS, HEAD), f32)
    seq = lax.axis_index(SEQ)
    position = seq * SLOTS + lax.broadcasted_iota(jnp.int32, (lines, SLOTS), 1)
    step = lax.broadcasted_iota(jnp.int32, (ROWS * lines, 8), 1)
    line_step = lax.broadcasted_iota(jnp.int32, (ROWS * lines, 8), 0) % STEPS
    step_seen = (step <= line_step) & (seq == 0)
    scores, step_scores, step_values = [], [], []
    for r in range(ROWS):
        q = qs[pl.ds(r, lines, stride=ROWS), :].astype(bf16)
        nk = nks[pl.ds(r, 8, stride=ROWS), :].astype(bf16)
        step_values.append(nvs[pl.ds(r, 8, stride=ROWS), :].astype(bf16))
        scores.append(jnp.where(position < lengths[requests[r]], dot_t(q, k_ref[r]), NEG))
        step_scores.append(dot_t(q, nk))
    s = jnp.concatenate(scores, axis=0)
    s2 = jnp.where(step_seen, jnp.concatenate(step_scores, axis=0), NEG)
    peak = jnp.maximum(jnp.max(s, axis=1, keepdims=True), jnp.max(s2, axis=1, keepdims=True))
    p = jnp.where(s > 0.5 * NEG, jnp.exp2((s - peak) * LOG2), 0.0)
    p2 = jnp.where(step_seen, jnp.exp2((s2 - peak) * LOG2), 0.0)
    total = jnp.sum(p, axis=1, keepdims=True) + jnp.sum(p2, axis=1, keepdims=True)
    p, p2 = p.astype(bf16), p2.astype(bf16)
    inverse = 1.0 / jnp.where(total > 0.0, total, 1.0)
    logs = log_total(peak, total)
    for r in range(ROWS):
        at = slice(r * lines, (r + 1) * lines)
        o = dot(p[at], v_ref[r]) + dot(p2[at], step_values[r])
        os[pl.ds(r, lines, stride=ROWS), :] = o * inverse[at]
        ls[pl.ds(r, lines, stride=ROWS), :] = jnp.broadcast_to(logs[at], (lines, HEAD))
    o = os[...].reshape(PEERS, 2, 8, HEAD)
    logs = ls[...].reshape(PEERS, 2, 8, HEAD)
    lane = lax.broadcasted_iota(jnp.int32, (PEERS, 8, HEAD), 2)
    stat = jnp.zeros((PEERS, 8, HEAD), f32)
    for b in range(2):
        out_ref[:, :, b * HEAD : (b + 1) * HEAD] = o[:, b].astype(bf16)
        for i, term in enumerate(terms(logs[:, b])):
            stat = jnp.where(lane == DEC_LANE + 3 * b + i, term, stat)
    out_ref[:, :, 2 * HEAD :] = stat.astype(bf16)


def prefill_kernel(q_ref, k_ref, v_ref, sk_ref, sv_ref, other_ref, dec_ref, out_ref, keys, values):
    seq, group = lax.axis_index(SEQ), lax.axis_index("group")
    own_k, own_v = sk_ref[...].astype(f32), sv_ref[...].astype(f32)
    far = other_ref[2 * CACHED :, :].astype(f32)
    far_k, far_v = far[:8], far[8:]
    first = jnp.full((8, HEAD), group, jnp.int32) == 0
    near_k = jnp.concatenate([jnp.where(first, own_k, far_k), jnp.where(first, far_k, own_k)], axis=0)
    near_v = jnp.concatenate([jnp.where(first, own_v, far_v), jnp.where(first, far_v, own_v)], axis=0)
    keys[0:CACHED, :] = k_ref[...]
    keys[CACHED : 2 * CACHED, :] = other_ref[0:CACHED, :]
    values[0:CACHED, :] = v_ref[...]
    values[CACHED : 2 * CACHED, :] = other_ref[CACHED : 2 * CACHED, :]
    keys[2 * CACHED :, :] = jnp.zeros((HEAD, HEAD), bf16)
    values[2 * CACHED :, :] = jnp.zeros((HEAD, HEAD), bf16)
    keys[2 * CACHED : 2 * CACHED + 16, :] = near_k.astype(bf16)
    values[2 * CACHED : 2 * CACHED + 16, :] = near_v.astype(bf16)
    for a in range(2):
        out_ref[:, a, :, DEC:NEW] = dec_ref[:, a, :, 0 : 2 * HEAD]
        out_ref[:, a, :, NEW : NEW + HEAD] = jnp.broadcast_to(own_k[None], (MATES, 8, HEAD)).astype(bf16)
        out_ref[:, a, :, NEW + HEAD :] = jnp.broadcast_to(own_v[None], (MATES, 8, HEAD)).astype(bf16)

    lane = lax.broadcasted_iota(jnp.int32, (PEERS, 8, HEAD), 2)
    index = lax.broadcasted_iota(jnp.int32, (HALF, HEAD), 1)
    query = group * HALF + lax.broadcasted_iota(jnp.int32, (HALF, HEAD), 0)
    seen = (index < 16) & (seq * 16 + index <= query)
    mine = pl.ds(pl.multiple_of(group * HALF, HALF), HALF)

    def scores(h):
        s = dot_t(q_ref[mine, h * HEAD : (h + 1) * HEAD], keys[...])
        return jnp.concatenate([s[:, : 2 * CACHED], jnp.where(seen, s[:, 2 * CACHED :], NEG)], axis=1)

    upcoming = scores(0)
    stat = jnp.concatenate([dec_ref[:, a, :, 2 * HEAD :].astype(f32) for a in range(2)], axis=0)
    for h in range(LOCAL):
        s = upcoming
        if h + 1 < LOCAL:
            upcoming = scores(h + 1)
        peak = jnp.max(s, axis=1, keepdims=True)
        edge = s[:, 2 * CACHED :]
        p = jnp.exp2((s[:, : 2 * CACHED] - peak) * LOG2)
        p = jnp.concatenate([p, jnp.where(seen, jnp.exp2((edge - peak) * LOG2), 0.0)], axis=1)
        total = jnp.sum(p, axis=1, keepdims=True)
        o = dot(p.astype(bf16), values[...])
        o = (o / total).reshape(PEERS, 8, HEAD)
        for a in range(2):
            out_ref[:, a, :, h * HEAD : (h + 1) * HEAD] = o[a * MATES : (a + 1) * MATES].astype(bf16)
        logs = jnp.broadcast_to(log_total(peak, total), (HALF, HEAD)).reshape(PEERS, 8, HEAD)
        for i, term in enumerate(terms(logs)):
            stat = jnp.where(lane == 3 * h + i, term, stat)
    for a in range(2):
        out_ref[:, a, :, STAT:DEC] = stat[a * MATES : (a + 1) * MATES].astype(bf16)


def combine_kernel(in_ref, out_ref, new_ref):
    new_ref[...] = in_ref[:, :, NEW:]
    t = in_ref[:, :, STAT:DEC].astype(f32).reshape(PEERS * 8, HEAD)
    logs = t + pltpu.roll(t, HEAD - 1, 1) + pltpu.roll(t, HEAD - 2, 1)
    logs = logs.reshape(PEERS, 8, HEAD)
    share = jnp.exp2(logs - jnp.max(logs, axis=0)[None])
    share = share / jnp.sum(share, axis=0)[None]
    for j in range(LOCAL + 2):
        lane = 3 * j if j < LOCAL else DEC_LANE + 3 * (j - LOCAL)
        at = j * HEAD if j < LOCAL else DEC + (j - LOCAL) * HEAD
        x = in_ref[:, :, at : at + HEAD].astype(f32)
        total = jnp.sum(x * share[:, :, lane : lane + 1], axis=0)
        out_ref[:, :, j * HEAD : (j + 1) * HEAD] = jnp.broadcast_to(total[None], (MATES, 8, HEAD)).astype(bf16)


def project_kernel(in_ref, w_ref, far_ref, out_ref, rows):
    pair = lax.axis_index("pair")
    rows[0 : HALF // 2, :] = in_ref[:, :, 0:STAT].astype(f32).reshape(HALF // 2, STAT)
    for h in range(LOCAL):
        for t in range(STEPS // 2):
            for b in range(2):
                at = HALF // 2 + t * ROWS + b * 8
                x = in_ref[h * STEPS // 2 + t, :, STAT + b * HEAD : STAT + (b + 1) * HEAD]
                rows[at : at + 8, h * HEAD : (h + 1) * HEAD] = x.astype(f32)
    x = rows[...].astype(bf16)

    def projected(ref):
        y = dot(x, ref[...])
        y = jnp.concatenate([y, jnp.zeros((2 * HEAD - y.shape[0], y.shape[1]), f32)], axis=0)
        return y.T.reshape(8, 32, 2 * HEAD).astype(bf16)

    out_ref[pl.ds(pl.multiple_of(pair * 8, 8), 8)] = projected(w_ref)
    out_ref[pl.ds(pl.multiple_of((1 - pair) * 8, 8), 8)] = projected(far_ref)


def last_kernel(in_ref, prefill_ref, decode_ref):
    for a in range(2):
        y = jnp.sum(in_ref[a * 8 : (a + 1) * 8].astype(f32), axis=0)
        prefill_ref[:, a * HEAD : (a + 1) * HEAD] = y[:, 0:HEAD].astype(bf16)
        steps = y[:, HEAD : 2 * HEAD].T
        for t in range(STEPS // 2):
            decode_ref[2 * t + a] = steps[t * ROWS : (t + 1) * ROWS].astype(bf16)


def landing_kernel(row_ref, own_ref, far_ref, keys_ref, values_ref):
    group = lax.axis_index("group")
    owner = lax.axis_index(SEQ) * 2 + group
    blocks, tokens = SPAN // BLOCK, SPAN // 2
    row = row_ref[...]
    column = jnp.broadcast_to(row.astype(f32), (blocks, blocks)).T.astype(jnp.int32)
    earlier = lax.broadcasted_iota(jnp.int32, (blocks, blocks), 0) < lax.broadcasted_iota(
        jnp.int32, (blocks, blocks), 1
    )
    same = (column == row) & earlier
    rank = jnp.sum(jnp.where(same, 1.0, 0.0), axis=0, keepdims=True)
    code = jnp.broadcast_to(jnp.where(row == owner, rank, -1.0), (16, blocks)).astype(bf16)
    token = lax.broadcasted_iota(jnp.int32, (blocks, tokens), 1)
    block = lax.broadcasted_iota(jnp.int32, (blocks, tokens), 0)
    line = lax.broadcasted_iota(jnp.int32, (16, tokens), 0)
    place_in = lax.broadcasted_iota(jnp.int32, (16, tokens), 1) % BLOCK

    def picked(side, ref):
        spread = (token // 8) * 4 + side * 2 + (token % 8) // BLOCK == block
        codes = dot(code, jnp.where(spread, 1.0, 0.0).astype(bf16))
        chosen = (codes == (line // BLOCK).astype(f32)) & (place_in == line % BLOCK)
        x = ref[...].astype(f32).reshape(tokens, 2 * HEAD).astype(bf16)
        return dot(jnp.where(chosen, 1.0, 0.0).astype(bf16), x)

    y = picked(group, own_ref) + picked(1 - group, far_ref)
    keys_ref[...] = y[:, :HEAD].astype(bf16)
    values_ref[...] = y[:, HEAD:].astype(bf16)


def cost(flops, moved, exps=0):
    return pl.CostEstimate(flops=flops, bytes_accessed=moved, transcendentals=exps)


SMEM = pl.BlockSpec(memory_space=pltpu.SMEM)
VMEM = pl.BlockSpec(memory_space=pltpu.VMEM)


def near(x):
    return pltpu.with_memory_space_constraint(x, pltpu.VMEM)


def swap(x, axis):
    return lax.all_to_all(x, axis, 0, 0, tiled=True)


def body(
    prefill_queries,
    cached_keys,
    cached_values,
    span_keys,
    span_values,
    out_weight,
    decode_queries,
    decode_keys,
    decode_values,
    new_keys,
    new_values,
    request_lengths,
    row_requests,
    block_table,
):
    mine = jnp.concatenate([cached_keys, cached_values, span_keys, span_values], axis=0)
    other = lax.ppermute(mine, "group", [(0, 1), (1, 0)])
    far_weight = lax.ppermute(out_weight, "pair", [(0, 1), (1, 0)])

    lines = LOCAL * STEPS * ROWS
    decoded = pl.pallas_call(
        decode_kernel,
        name="decode",
        out_shape=jax.ShapeDtypeStruct((PEERS, 8, 3 * HEAD), bf16),
        in_specs=[SMEM] * 2 + [VMEM] * 5,
        out_specs=VMEM,
        scratch_shapes=[pltpu.VMEM((lines, HEAD), f32)] * 3 + [pltpu.VMEM((2 * STEPS * ROWS, HEAD), f32)] * 2,
        cost_estimate=cost(2 * 2 * 512 * SLOTS * HEAD * 8, 3 << 20, 512 * SLOTS),
    )(request_lengths, row_requests, decode_queries, decode_keys, decode_values, new_keys, new_values)

    packed = pl.pallas_call(
        prefill_kernel,
        name="prefill",
        out_shape=jax.ShapeDtypeStruct((MATES, 2, 8, WIDE), bf16),
        in_specs=[VMEM] * 7,
        out_specs=VMEM,
        scratch_shapes=[pltpu.VMEM((KEYS, HEAD), bf16)] * 2,
        cost_estimate=cost(4 * HALF * LOCAL * KEYS * HEAD, 4 << 20, HALF * LOCAL * KEYS),
    )(
        near(prefill_queries),
        near(cached_keys),
        near(cached_values),
        span_keys,
        span_values,
        near(other),
        decoded.reshape(MATES, 2, 8, 3 * HEAD),
    )

    packed, far_weight = lax.optimization_barrier((packed, far_weight))
    arrived = swap(packed.reshape(PEERS, 8, WIDE), SEQ)
    attention, new_own = pl.pallas_call(
        combine_kernel,
        name="combine",
        out_shape=(
            jax.ShapeDtypeStruct((MATES, 8, THIN), bf16),
            jax.ShapeDtypeStruct((PEERS, 8, 2 * HEAD), bf16),
        ),
        in_specs=[VMEM],
        out_specs=(VMEM, VMEM),
        cost_estimate=cost(1 << 20, 2 << 20),
    )(near(arrived))
    new_far = lax.ppermute(new_own, "group", [(0, 1), (1, 0)])
    attention = swap(attention, SEQ[:2])
    landed_keys, landed_values = pl.pallas_call(
        landing_kernel,
        name="landing",
        out_shape=(jax.ShapeDtypeStruct((16, HEAD), bf16), jax.ShapeDtypeStruct((16, HEAD), bf16)),
        in_specs=[VMEM] * 3,
        out_specs=(VMEM, VMEM),
        cost_estimate=cost(1 << 22, 1 << 19),
    )(block_table.reshape(1, -1), near(new_own), near(new_far))
    attention, landed_keys, landed_values = lax.optimization_barrier((attention, landed_keys, landed_values))
    columns = out_weight.shape[1]
    partial = pl.pallas_call(
        project_kernel,
        name="project",
        out_shape=jax.ShapeDtypeStruct((16, columns // 8, 2 * HEAD), bf16),
        in_specs=[VMEM] * 3,
        out_specs=VMEM,
        scratch_shapes=[pltpu.VMEM(((HALF + STEPS * ROWS) // 2, STAT), f32)],
        cost_estimate=cost(2 * 320 * STAT * columns, 2 << 20),
    )(near(attention), out_weight, near(far_weight))
    partial = swap(partial, ("pair", "tensor"))
    prefill_out, decode_out = pl.pallas_call(
        last_kernel,
        name="last",
        out_shape=(
            jax.ShapeDtypeStruct((columns // 8, HALF), bf16),
            jax.ShapeDtypeStruct((STEPS, ROWS, columns // 8), bf16),
        ),
        in_specs=[VMEM],
        out_specs=(VMEM, VMEM),
        cost_estimate=cost(1 << 18, 1 << 19),
    )(near(partial))
    shape = (1, 4, BLOCK, HEAD)
    return (prefill_out.T, decode_out, landed_keys.reshape(shape), landed_values.reshape(shape))


def solution(mesh):
    torus = Mesh(
        mesh.devices.reshape(4, 4, 2, mesh.shape["tensor"], mesh.shape["group"]),
        (*SEQ, "tensor", "group"),
    )
    in_specs = (
        P(None, "tensor"),
        P(SEQ_GROUP, "tensor"),
        P(SEQ_GROUP, "tensor"),
        P(SEQ_GROUP, "tensor"),
        P(SEQ_GROUP, "tensor"),
        P("tensor", SEQ),
        P(None, "group", "tensor"),
        P("group", SEQ, "tensor"),
        P("group", SEQ, "tensor"),
        P(None, "group", "tensor"),
        P(None, "group", "tensor"),
        P(),
        P("group"),
        P(),
    )
    out_specs = (
        P("group", SEQ_TENSOR),
        P(None, "group", SEQ_TENSOR),
        P(SEQ_GROUP, None, None, "tensor"),
        P(SEQ_GROUP, None, None, "tensor"),
    )
    return jax.shard_map(body, mesh=torus, in_specs=in_specs, out_specs=out_specs, check_vma=False)
```

```python
import math

import jax
import jax.numpy as jnp
from jax import lax
from jax.experimental import pallas as pl
from jax.experimental.pallas import tpu as pltpu
from jax.sharding import Mesh
from jax.sharding import PartitionSpec as P


HEAD = 128
SPAN = 512
BLOCK = 4
STEPS = 4
SEQ = ("seq_0", "seq_1", "pair")
SEQ_GROUP = (*SEQ, "group")
SEQ_TENSOR = (*SEQ, "tensor")

PEERS = 32
MATES = PEERS // 2
LOCAL = 8
ROWS = 16
SLOTS = 256
CACHED = 1024
HALF = 256
KEYS = 2 * CACHED + 128
STAT = LOCAL * HEAD
DEC = STAT + HEAD
NEW = DEC + 2 * HEAD
WIDE = NEW + 2 * HEAD
THIN = STAT + 2 * HEAD
DEC_LANE = 32

NEG = -1e30
LOG2 = HEAD**-0.5 * math.log2(math.e)
bf16 = jnp.bfloat16
f32 = jnp.float32


def log_total(peak, total):
    safe = jnp.where(total > 0.0, total, 1.0)
    return jnp.where(total > 0.0, peak * LOG2 + jnp.log2(safe), NEG)


def terms(x):
    first = x.astype(bf16).astype(f32)
    rest = x - first
    second = rest.astype(bf16).astype(f32)
    return (first, second, rest - second)


def dot_t(a, b):
    return lax.dot_general(a, b, (((1,), (1,)), ((), ())), preferred_element_type=f32)


def dot(a, b):
    return lax.dot_general(a, b, (((1,), (0,)), ((), ())), preferred_element_type=f32)


def decode_kernel(lengths, requests, q_ref, k_ref, v_ref, nk_ref, nv_ref, out_ref, qs, os, ls, nks, nvs):
    lines = LOCAL * STEPS
    for h in range(LOCAL):
        for t in range(STEPS):
            at = (h * STEPS + t) * ROWS
            qs[at : at + ROWS, :] = q_ref[t, :, h * HEAD : (h + 1) * HEAD].astype(f32)
    for u in range(STEPS):
        nks[u * ROWS : (u + 1) * ROWS, :] = nk_ref[u].astype(f32)
        nvs[u * ROWS : (u + 1) * ROWS, :] = nv_ref[u].astype(f32)
    nks[STEPS * ROWS :, :] = jnp.zeros((STEPS * ROWS, HEAD), f32)
    nvs[STEPS * ROWS :, :] = jnp.zeros((STEPS * ROWS, HEAD), f32)
    seq = lax.axis_index(SEQ)
    position = seq * SLOTS + lax.broadcasted_iota(jnp.int32, (lines, SLOTS), 1)
    step = lax.broadcasted_iota(jnp.int32, (ROWS * lines, 8), 1)
    line_step = lax.broadcasted_iota(jnp.int32, (ROWS * lines, 8), 0) % STEPS
    step_seen = (step <= line_step) & (seq == 0)
    scores, step_scores, step_values = [], [], []
    for r in range(ROWS):
        q = qs[pl.ds(r, lines, stride=ROWS), :].astype(bf16)
        nk = nks[pl.ds(r, 8, stride=ROWS), :].astype(bf16)
        step_values.append(nvs[pl.ds(r, 8, stride=ROWS), :].astype(bf16))
        scores.append(jnp.where(position < lengths[requests[r]], dot_t(q, k_ref[r]), NEG))
        step_scores.append(dot_t(q, nk))
    s = jnp.concatenate(scores, axis=0)
    s2 = jnp.where(step_seen, jnp.concatenate(step_scores, axis=0), NEG)
    peak = jnp.maximum(jnp.max(s, axis=1, keepdims=True), jnp.max(s2, axis=1, keepdims=True))
    p = jnp.where(s > 0.5 * NEG, jnp.exp2((s - peak) * LOG2), 0.0)
    p2 = jnp.where(step_seen, jnp.exp2((s2 - peak) * LOG2), 0.0)
    total = jnp.sum(p, axis=1, keepdims=True) + jnp.sum(p2, axis=1, keepdims=True)
    p, p2 = p.astype(bf16), p2.astype(bf16)
    inverse = 1.0 / jnp.where(total > 0.0, total, 1.0)
    logs = log_total(peak, total)
    for r in range(ROWS):
        at = slice(r * lines, (r + 1) * lines)
        o = dot(p[at], v_ref[r]) + dot(p2[at], step_values[r])
        os[pl.ds(r, lines, stride=ROWS), :] = o * inverse[at]
        ls[pl.ds(r, lines, stride=ROWS), :] = jnp.broadcast_to(logs[at], (lines, HEAD))
    o = os[...].reshape(PEERS, 2, 8, HEAD)
    logs = ls[...].reshape(PEERS, 2, 8, HEAD)
    lane = lax.broadcasted_iota(jnp.int32, (PEERS, 8, HEAD), 2)
    stat = jnp.zeros((PEERS, 8, HEAD), f32)
    for b in range(2):
        out_ref[:, :, b * HEAD : (b + 1) * HEAD] = o[:, b].astype(bf16)
        for i, term in enumerate(terms(logs[:, b])):
            stat = jnp.where(lane == DEC_LANE + 3 * b + i, term, stat)
    out_ref[:, :, 2 * HEAD :] = stat.astype(bf16)


def prefill_kernel(q_ref, k_ref, v_ref, sk_ref, sv_ref, other_ref, dec_ref, out_ref, keys, values):
    seq, group = lax.axis_index(SEQ), lax.axis_index("group")
    own_k, own_v = sk_ref[...].astype(f32), sv_ref[...].astype(f32)
    far = other_ref[2 * CACHED :, :].astype(f32)
    far_k, far_v = far[:8], far[8:]
    first = jnp.full((8, HEAD), group, jnp.int32) == 0
    near_k = jnp.concatenate([jnp.where(first, own_k, far_k), jnp.where(first, far_k, own_k)], axis=0)
    near_v = jnp.concatenate([jnp.where(first, own_v, far_v), jnp.where(first, far_v, own_v)], axis=0)
    keys[0:CACHED, :] = k_ref[...]
    keys[CACHED : 2 * CACHED, :] = other_ref[0:CACHED, :]
    values[0:CACHED, :] = v_ref[...]
    values[CACHED : 2 * CACHED, :] = other_ref[CACHED : 2 * CACHED, :]
    keys[2 * CACHED :, :] = jnp.zeros((HEAD, HEAD), bf16)
    values[2 * CACHED :, :] = jnp.zeros((HEAD, HEAD), bf16)
    keys[2 * CACHED : 2 * CACHED + 16, :] = near_k.astype(bf16)
    values[2 * CACHED : 2 * CACHED + 16, :] = near_v.astype(bf16)
    for a in range(2):
        out_ref[:, a, :, DEC:NEW] = dec_ref[:, a, :, 0 : 2 * HEAD]
        out_ref[:, a, :, NEW : NEW + HEAD] = jnp.broadcast_to(own_k[None], (MATES, 8, HEAD)).astype(bf16)
        out_ref[:, a, :, NEW + HEAD :] = jnp.broadcast_to(own_v[None], (MATES, 8, HEAD)).astype(bf16)

    lane = lax.broadcasted_iota(jnp.int32, (PEERS, 8, HEAD), 2)
    index = lax.broadcasted_iota(jnp.int32, (HALF, HEAD), 1)
    query = group * HALF + lax.broadcasted_iota(jnp.int32, (HALF, HEAD), 0)
    seen = (index < 16) & (seq * 16 + index <= query)
    mine = pl.ds(pl.multiple_of(group * HALF, HALF), HALF)

    def scores(h):
        s = dot_t(q_ref[mine, h * HEAD : (h + 1) * HEAD], keys[...])
        return jnp.concatenate([s[:, : 2 * CACHED], jnp.where(seen, s[:, 2 * CACHED :], NEG)], axis=1)

    upcoming = scores(0)
    stat = jnp.concatenate([dec_ref[:, a, :, 2 * HEAD :].astype(f32) for a in range(2)], axis=0)
    for h in range(LOCAL):
        s = upcoming
        if h + 1 < LOCAL:
            upcoming = scores(h + 1)
        peak = jnp.max(s, axis=1, keepdims=True)
        edge = s[:, 2 * CACHED :]
        p = jnp.exp2((s[:, : 2 * CACHED] - peak) * LOG2)
        p = jnp.concatenate([p, jnp.where(seen, jnp.exp2((edge - peak) * LOG2), 0.0)], axis=1)
        total = jnp.sum(p, axis=1, keepdims=True)
        o = dot(p.astype(bf16), values[...])
        o = (o / total).reshape(PEERS, 8, HEAD)
        for a in range(2):
            out_ref[:, a, :, h * HEAD : (h + 1) * HEAD] = o[a * MATES : (a + 1) * MATES].astype(bf16)
        logs = jnp.broadcast_to(log_total(peak, total), (HALF, HEAD)).reshape(PEERS, 8, HEAD)
        for i, term in enumerate(terms(logs)):
            stat = jnp.where(lane == 3 * h + i, term, stat)
    for a in range(2):
        out_ref[:, a, :, STAT:DEC] = stat[a * MATES : (a + 1) * MATES].astype(bf16)


def combine_kernel(in_ref, out_ref, new_ref):
    new_ref[...] = in_ref[:, :, NEW:]
    t = in_ref[:, :, STAT:DEC].astype(f32).reshape(PEERS * 8, HEAD)
    logs = t + pltpu.roll(t, HEAD - 1, 1) + pltpu.roll(t, HEAD - 2, 1)
    logs = logs.reshape(PEERS, 8, HEAD)
    share = jnp.exp2(logs - jnp.max(logs, axis=0)[None])
    share = share / jnp.sum(share, axis=0)[None]
    for j in range(LOCAL + 2):
        lane = 3 * j if j < LOCAL else DEC_LANE + 3 * (j - LOCAL)
        at = j * HEAD if j < LOCAL else DEC + (j - LOCAL) * HEAD
        x = in_ref[:, :, at : at + HEAD].astype(f32)
        total = jnp.sum(x * share[:, :, lane : lane + 1], axis=0)
        out_ref[:, :, j * HEAD : (j + 1) * HEAD] = jnp.broadcast_to(total[None], (MATES, 8, HEAD)).astype(bf16)


def project_kernel(in_ref, w_ref, far_ref, out_ref, rows):
    pair = lax.axis_index("pair")
    rows[0 : HALF // 2, :] = in_ref[:, :, 0:STAT].astype(f32).reshape(HALF // 2, STAT)
    for h in range(LOCAL):
        for t in range(STEPS // 2):
            for b in range(2):
                at = HALF // 2 + t * ROWS + b * 8
                x = in_ref[h * STEPS // 2 + t, :, STAT + b * HEAD : STAT + (b + 1) * HEAD]
                rows[at : at + 8, h * HEAD : (h + 1) * HEAD] = x.astype(f32)
    x = rows[...].astype(bf16)

    def projected(ref):
        y = dot(x, ref[...])
        y = jnp.concatenate([y, jnp.zeros((2 * HEAD - y.shape[0], y.shape[1]), f32)], axis=0)
        return y.astype(bf16).T.reshape(8, 32, 2 * HEAD)

    out_ref[pl.ds(pl.multiple_of(pair * 8, 8), 8)] = projected(w_ref)
    out_ref[pl.ds(pl.multiple_of((1 - pair) * 8, 8), 8)] = projected(far_ref)


def last_kernel(in_ref, prefill_ref, decode_ref):
    for a in range(2):
        y = jnp.sum(in_ref[a * 8 : (a + 1) * 8].astype(f32), axis=0)
        prefill_ref[:, a * HEAD : (a + 1) * HEAD] = y[:, 0:HEAD].astype(bf16)
        steps = y[:, HEAD : 2 * HEAD].T
        for t in range(STEPS // 2):
            decode_ref[2 * t + a] = steps[t * ROWS : (t + 1) * ROWS].astype(bf16)


def landing_kernel(row_ref, own_ref, far_ref, keys_ref, values_ref):
    group = lax.axis_index("group")
    owner = lax.axis_index(SEQ) * 2 + group
    blocks, tokens = SPAN // BLOCK, SPAN // 2
    row = row_ref[...]
    column = jnp.broadcast_to(row.astype(f32), (blocks, blocks)).T.astype(jnp.int32)
    earlier = lax.broadcasted_iota(jnp.int32, (blocks, blocks), 0) < lax.broadcasted_iota(
        jnp.int32, (blocks, blocks), 1
    )
    same = (column == row) & earlier
    rank = jnp.sum(jnp.where(same, 1.0, 0.0), axis=0, keepdims=True)
    code = jnp.broadcast_to(jnp.where(row == owner, rank, -1.0), (16, blocks)).astype(bf16)
    token = lax.broadcasted_iota(jnp.int32, (blocks, tokens), 1)
    block = lax.broadcasted_iota(jnp.int32, (blocks, tokens), 0)
    line = lax.broadcasted_iota(jnp.int32, (16, tokens), 0)
    place_in = lax.broadcasted_iota(jnp.int32, (16, tokens), 1) % BLOCK

    def picked(side, ref):
        spread = (token // 8) * 4 + side * 2 + (token % 8) // BLOCK == block
        codes = dot(code, jnp.where(spread, 1.0, 0.0).astype(bf16))
        chosen = (codes == (line // BLOCK).astype(f32)) & (place_in == line % BLOCK)
        x = ref[...].astype(f32).reshape(tokens, 2 * HEAD).astype(bf16)
        return dot(jnp.where(chosen, 1.0, 0.0).astype(bf16), x)

    y = picked(group, own_ref) + picked(1 - group, far_ref)
    keys_ref[...] = y[:, :HEAD].astype(bf16)
    values_ref[...] = y[:, HEAD:].astype(bf16)


def cost(flops, moved, exps=0):
    return pl.CostEstimate(flops=flops, bytes_accessed=moved, transcendentals=exps)


SMEM = pl.BlockSpec(memory_space=pltpu.SMEM)
VMEM = pl.BlockSpec(memory_space=pltpu.VMEM)


def near(x):
    return pltpu.with_memory_space_constraint(x, pltpu.VMEM)


def swap(x, axis):
    return lax.all_to_all(x, axis, 0, 0, tiled=True)


def body(
    prefill_queries,
    cached_keys,
    cached_values,
    span_keys,
    span_values,
    out_weight,
    decode_queries,
    decode_keys,
    decode_values,
    new_keys,
    new_values,
    request_lengths,
    row_requests,
    block_table,
):
    mine = jnp.concatenate([cached_keys, cached_values, span_keys, span_values], axis=0)
    far_weight = lax.ppermute(out_weight, "pair", [(0, 1), (1, 0)])
    other = lax.ppermute(mine, "group", [(0, 1), (1, 0)])

    lines = LOCAL * STEPS * ROWS
    decoded = pl.pallas_call(
        decode_kernel,
        name="decode",
        out_shape=jax.ShapeDtypeStruct((PEERS, 8, 3 * HEAD), bf16),
        in_specs=[SMEM] * 2 + [VMEM] * 5,
        out_specs=VMEM,
        scratch_shapes=[pltpu.VMEM((lines, HEAD), f32)] * 3 + [pltpu.VMEM((2 * STEPS * ROWS, HEAD), f32)] * 2,
        cost_estimate=cost(2 * 2 * 512 * SLOTS * HEAD * 8, 3 << 20, 512 * SLOTS),
    )(request_lengths, row_requests, decode_queries, decode_keys, decode_values, new_keys, new_values)

    packed = pl.pallas_call(
        prefill_kernel,
        name="prefill",
        out_shape=jax.ShapeDtypeStruct((MATES, 2, 8, WIDE), bf16),
        in_specs=[VMEM] * 7,
        out_specs=VMEM,
        scratch_shapes=[pltpu.VMEM((KEYS, HEAD), bf16)] * 2,
        cost_estimate=cost(4 * HALF * LOCAL * KEYS * HEAD, 4 << 20, HALF * LOCAL * KEYS),
    )(
        near(prefill_queries),
        near(cached_keys),
        near(cached_values),
        span_keys,
        span_values,
        near(other),
        decoded.reshape(MATES, 2, 8, 3 * HEAD),
    )

    packed, far_weight = lax.optimization_barrier((packed, far_weight))
    arrived = swap(packed.reshape(PEERS, 8, WIDE), SEQ)
    arrived, late_weight = lax.optimization_barrier((arrived, out_weight))
    attention, new_own = pl.pallas_call(
        combine_kernel,
        name="combine",
        out_shape=(
            jax.ShapeDtypeStruct((MATES, 8, THIN), bf16),
            jax.ShapeDtypeStruct((PEERS, 8, 2 * HEAD), bf16),
        ),
        in_specs=[VMEM],
        out_specs=(VMEM, VMEM),
        cost_estimate=cost(1 << 20, 2 << 20),
    )(near(arrived))
    new_far = lax.ppermute(new_own, "group", [(0, 1), (1, 0)])
    attention = swap(attention, SEQ[:2])
    landed_keys, landed_values = pl.pallas_call(
        landing_kernel,
        name="landing",
        out_shape=(jax.ShapeDtypeStruct((16, HEAD), bf16), jax.ShapeDtypeStruct((16, HEAD), bf16)),
        in_specs=[VMEM] * 3,
        out_specs=(VMEM, VMEM),
        cost_estimate=cost(1 << 22, 1 << 19),
    )(block_table.reshape(1, -1), near(new_own), near(new_far))
    attention, landed_keys, landed_values = lax.optimization_barrier((attention, landed_keys, landed_values))
    columns = out_weight.shape[1]
    near_weight = near(late_weight)
    partial = pl.pallas_call(
        project_kernel,
        name="project",
        out_shape=jax.ShapeDtypeStruct((16, columns // 8, 2 * HEAD), bf16),
        in_specs=[VMEM] * 3,
        out_specs=VMEM,
        scratch_shapes=[pltpu.VMEM(((HALF + STEPS * ROWS) // 2, STAT), f32)],
        cost_estimate=cost(2 * 320 * STAT * columns, 2 << 20),
    )(near(attention), near_weight, near(far_weight))
    partial = swap(partial, ("pair", "tensor"))
    prefill_out, decode_out = pl.pallas_call(
        last_kernel,
        name="last",
        out_shape=(
            jax.ShapeDtypeStruct((columns // 8, HALF), bf16),
            jax.ShapeDtypeStruct((STEPS, ROWS, columns // 8), bf16),
        ),
        in_specs=[VMEM],
        out_specs=(VMEM, VMEM),
        cost_estimate=cost(1 << 18, 1 << 19),
    )(near(partial))
    shape = (1, 4, BLOCK, HEAD)
    return (prefill_out.T, decode_out, landed_keys.reshape(shape), landed_values.reshape(shape))


def solution(mesh):
    torus = Mesh(
        mesh.devices.reshape(4, 4, 2, mesh.shape["tensor"], mesh.shape["group"]),
        (*SEQ, "tensor", "group"),
    )
    in_specs = (
        P(None, "tensor"),
        P(SEQ_GROUP, "tensor"),
        P(SEQ_GROUP, "tensor"),
        P(SEQ_GROUP, "tensor"),
        P(SEQ_GROUP, "tensor"),
        P("tensor", SEQ),
        P(None, "group", "tensor"),
        P("group", SEQ, "tensor"),
        P("group", SEQ, "tensor"),
        P(None, "group", "tensor"),
        P(None, "group", "tensor"),
        P(),
        P("group"),
        P(),
    )
    out_specs = (
        P("group", SEQ_TENSOR),
        P(None, "group", SEQ_TENSOR),
        P(SEQ_GROUP, None, None, "tensor"),
        P(SEQ_GROUP, None, None, "tensor"),
    )
    return jax.shard_map(body, mesh=torus, in_specs=in_specs, out_specs=out_specs, check_vma=False)
```

```python
import math

import jax
import jax.numpy as jnp
from jax import lax
from jax.experimental import pallas as pl
from jax.experimental.pallas import tpu as pltpu
from jax.sharding import Mesh
from jax.sharding import PartitionSpec as P


HEAD = 128
SPAN = 512
BLOCK = 4
STEPS = 4
SEQ = ("seq_0", "seq_1", "pair")
SEQ_GROUP = (*SEQ, "group")
SEQ_TENSOR = (*SEQ, "tensor")

PEERS = 32
MATES = PEERS // 2
LOCAL = 8
ROWS = 16
SLOTS = 256
CACHED = 1024
HALF = 256
KEYS = 2 * CACHED + 128
STAT = LOCAL * HEAD
DEC = STAT + HEAD
NEW = DEC + 2 * HEAD
WIDE = NEW + 2 * HEAD
THIN = STAT + 2 * HEAD
DEC_LANE = 32

NEG = -1e30
LOG2 = HEAD**-0.5 * math.log2(math.e)
bf16 = jnp.bfloat16
f32 = jnp.float32


def log_total(peak, total):
    safe = jnp.where(total > 0.0, total, 1.0)
    return jnp.where(total > 0.0, peak * LOG2 + jnp.log2(safe), NEG)


def terms(x):
    first = x.astype(bf16).astype(f32)
    rest = x - first
    second = rest.astype(bf16).astype(f32)
    return (first, second, rest - second)


def dot_t(a, b):
    return lax.dot_general(a, b, (((1,), (1,)), ((), ())), preferred_element_type=f32)


def dot(a, b):
    return lax.dot_general(a, b, (((1,), (0,)), ((), ())), preferred_element_type=f32)


def decode_kernel(lengths, requests, q_ref, k_ref, v_ref, nk_ref, nv_ref, out_ref, qs, os, ls, nks, nvs):
    lines = LOCAL * STEPS
    for h in range(LOCAL):
        for t in range(STEPS):
            at = (h * STEPS + t) * ROWS
            qs[at : at + ROWS, :] = q_ref[t, :, h * HEAD : (h + 1) * HEAD].astype(f32)
    for u in range(STEPS):
        nks[u * ROWS : (u + 1) * ROWS, :] = nk_ref[u].astype(f32)
        nvs[u * ROWS : (u + 1) * ROWS, :] = nv_ref[u].astype(f32)
    nks[STEPS * ROWS :, :] = jnp.zeros((STEPS * ROWS, HEAD), f32)
    nvs[STEPS * ROWS :, :] = jnp.zeros((STEPS * ROWS, HEAD), f32)
    seq = lax.axis_index(SEQ)
    position = seq * SLOTS + lax.broadcasted_iota(jnp.int32, (lines, SLOTS), 1)
    step = lax.broadcasted_iota(jnp.int32, (ROWS * lines, 8), 1)
    line_step = lax.broadcasted_iota(jnp.int32, (ROWS * lines, 8), 0) % STEPS
    step_seen = (step <= line_step) & (seq == 0)
    scores, step_scores, step_values = [], [], []
    for r in range(ROWS):
        q = qs[pl.ds(r, lines, stride=ROWS), :].astype(bf16)
        nk = nks[pl.ds(r, 8, stride=ROWS), :].astype(bf16)
        step_values.append(nvs[pl.ds(r, 8, stride=ROWS), :].astype(bf16))
        scores.append(jnp.where(position < lengths[requests[r]], dot_t(q, k_ref[r]), NEG))
        step_scores.append(dot_t(q, nk))
    s = jnp.concatenate(scores, axis=0)
    s2 = jnp.where(step_seen, jnp.concatenate(step_scores, axis=0), NEG)
    peak = jnp.maximum(jnp.max(s, axis=1, keepdims=True), jnp.max(s2, axis=1, keepdims=True))
    p = jnp.where(s > 0.5 * NEG, jnp.exp2((s - peak) * LOG2), 0.0)
    p2 = jnp.where(step_seen, jnp.exp2((s2 - peak) * LOG2), 0.0)
    total = jnp.sum(p, axis=1, keepdims=True) + jnp.sum(p2, axis=1, keepdims=True)
    p, p2 = p.astype(bf16), p2.astype(bf16)
    inverse = 1.0 / jnp.where(total > 0.0, total, 1.0)
    logs = log_total(peak, total)
    for r in range(ROWS):
        at = slice(r * lines, (r + 1) * lines)
        o = dot(p[at], v_ref[r]) + dot(p2[at], step_values[r])
        os[pl.ds(r, lines, stride=ROWS), :] = o * inverse[at]
        ls[pl.ds(r, lines, stride=ROWS), :] = jnp.broadcast_to(logs[at], (lines, HEAD))
    o = os[...].reshape(PEERS, 2, 8, HEAD)
    logs = ls[...].reshape(PEERS, 2, 8, HEAD)
    lane = lax.broadcasted_iota(jnp.int32, (PEERS, 8, HEAD), 2)
    stat = jnp.zeros((PEERS, 8, HEAD), f32)
    for b in range(2):
        out_ref[:, :, b * HEAD : (b + 1) * HEAD] = o[:, b].astype(bf16)
        for i, term in enumerate(terms(logs[:, b])):
            stat = jnp.where(lane == DEC_LANE + 3 * b + i, term, stat)
    out_ref[:, :, 2 * HEAD :] = stat.astype(bf16)


def prefill_kernel(q_ref, k_ref, v_ref, sk_ref, sv_ref, other_ref, dec_ref, out_ref, keys, values):
    seq, group = lax.axis_index(SEQ), lax.axis_index("group")
    own_k, own_v = sk_ref[...].astype(f32), sv_ref[...].astype(f32)
    far = other_ref[2 * CACHED :, :].astype(f32)
    far_k, far_v = far[:8], far[8:]
    first = jnp.full((8, HEAD), group, jnp.int32) == 0
    near_k = jnp.concatenate([jnp.where(first, own_k, far_k), jnp.where(first, far_k, own_k)], axis=0)
    near_v = jnp.concatenate([jnp.where(first, own_v, far_v), jnp.where(first, far_v, own_v)], axis=0)
    keys[0:CACHED, :] = k_ref[...]
    keys[CACHED : 2 * CACHED, :] = other_ref[0:CACHED, :]
    values[:, HEAD:] = jnp.ones((KEYS, HEAD), bf16)
    values[0:CACHED, 0:HEAD] = v_ref[...]
    values[CACHED : 2 * CACHED, 0:HEAD] = other_ref[CACHED : 2 * CACHED, :]
    keys[2 * CACHED :, :] = jnp.zeros((HEAD, HEAD), bf16)
    values[2 * CACHED :, 0:HEAD] = jnp.zeros((HEAD, HEAD), bf16)
    keys[2 * CACHED : 2 * CACHED + 16, :] = near_k.astype(bf16)
    values[2 * CACHED : 2 * CACHED + 16, 0:HEAD] = near_v.astype(bf16)
    for a in range(2):
        out_ref[:, a, :, DEC:NEW] = dec_ref[:, a, :, 0 : 2 * HEAD]
        out_ref[:, a, :, NEW : NEW + HEAD] = jnp.broadcast_to(own_k[None], (MATES, 8, HEAD)).astype(bf16)
        out_ref[:, a, :, NEW + HEAD :] = jnp.broadcast_to(own_v[None], (MATES, 8, HEAD)).astype(bf16)

    lane = lax.broadcasted_iota(jnp.int32, (PEERS, 8, HEAD), 2)
    index = lax.broadcasted_iota(jnp.int32, (HALF, HEAD), 1)
    query = group * HALF + lax.broadcasted_iota(jnp.int32, (HALF, HEAD), 0)
    seen = (index < 16) & (seq * 16 + index <= query)
    mine = pl.ds(pl.multiple_of(group * HALF, HALF), HALF)

    def scores(h):
        s = dot_t(q_ref[mine, h * HEAD : (h + 1) * HEAD], keys[...])
        return jnp.concatenate([s[:, : 2 * CACHED], jnp.where(seen, s[:, 2 * CACHED :], NEG)], axis=1)

    upcoming = scores(0)
    stat = jnp.concatenate([dec_ref[:, a, :, 2 * HEAD :].astype(f32) for a in range(2)], axis=0)
    for h in range(LOCAL):
        s = upcoming
        if h + 1 < LOCAL:
            upcoming = scores(h + 1)
        peak = jnp.max(s, axis=1, keepdims=True)
        edge = s[:, 2 * CACHED :]
        p = jnp.exp2((s[:, : 2 * CACHED] - peak) * LOG2)
        p = jnp.concatenate([p, jnp.where(seen, jnp.exp2((edge - peak) * LOG2), 0.0)], axis=1)
        o = dot(p.astype(bf16), values[...])
        o, total = o[:, :HEAD], o[:, HEAD:]
        o = (o / total).reshape(PEERS, 8, HEAD)
        for a in range(2):
            out_ref[:, a, :, h * HEAD : (h + 1) * HEAD] = o[a * MATES : (a + 1) * MATES].astype(bf16)
        logs = log_total(peak, total).reshape(PEERS, 8, HEAD)
        for i, term in enumerate(terms(logs)):
            stat = jnp.where(lane == 3 * h + i, term, stat)
    for a in range(2):
        out_ref[:, a, :, STAT:DEC] = stat[a * MATES : (a + 1) * MATES].astype(bf16)


def combine_kernel(in_ref, out_ref, new_ref):
    new_ref[...] = in_ref[:, :, NEW:]
    t = in_ref[:, :, STAT:DEC].astype(f32).reshape(PEERS * 8, HEAD)
    logs = t + pltpu.roll(t, HEAD - 1, 1) + pltpu.roll(t, HEAD - 2, 1)
    logs = logs.reshape(PEERS, 8, HEAD)
    share = jnp.exp2(logs - jnp.max(logs, axis=0)[None])
    share = share / jnp.sum(share, axis=0)[None]
    for j in range(LOCAL + 2):
        lane = 3 * j if j < LOCAL else DEC_LANE + 3 * (j - LOCAL)
        at = j * HEAD if j < LOCAL else DEC + (j - LOCAL) * HEAD
        x = in_ref[:, :, at : at + HEAD].astype(f32)
        total = jnp.sum(x * share[:, :, lane : lane + 1], axis=0)
        out_ref[:, :, j * HEAD : (j + 1) * HEAD] = jnp.broadcast_to(total[None], (MATES, 8, HEAD)).astype(bf16)


def project_kernel(in_ref, w_ref, far_ref, out_ref, rows):
    pair = lax.axis_index("pair")
    rows[0 : HALF // 2, :] = in_ref[:, :, 0:STAT].astype(f32).reshape(HALF // 2, STAT)
    for h in range(LOCAL):
        for t in range(STEPS // 2):
            for b in range(2):
                at = HALF // 2 + t * ROWS + b * 8
                x = in_ref[h * STEPS // 2 + t, :, STAT + b * HEAD : STAT + (b + 1) * HEAD]
                rows[at : at + 8, h * HEAD : (h + 1) * HEAD] = x.astype(f32)
    x = rows[...].astype(bf16)

    for ref, side in ((w_ref, pair), (far_ref, 1 - pair)):
        y = dot(x, ref[...])
        y = jnp.concatenate([y, jnp.zeros((2 * HEAD - y.shape[0], y.shape[1]), f32)], axis=0)
        y = y.astype(bf16).T
        steps = y[:, HEAD:].astype(f32).reshape(8, 4, 8, HEAD)
        packed = steps[:, 0].reshape(8 * 8, HEAD) + sum(pltpu.roll(steps[:, g].reshape(8 * 8, HEAD), 32 * g, 1) for g in range(1, 4))
        peers = pl.ds(pl.multiple_of(side * 8, 8), 8)
        out_ref[peers, 0:32, :] = y[:, :HEAD].reshape(8, 32, HEAD)
        out_ref[peers, 32:40, :] = packed.reshape(8, 8, HEAD).astype(bf16)


def last_kernel(in_ref, prefill_ref, decode_ref):
    for a in range(2):
        y = jnp.sum(in_ref[a * 8 : (a + 1) * 8].astype(f32), axis=0)
        prefill_ref[:, a * HEAD : (a + 1) * HEAD] = y[0:32].astype(bf16)
        steps = [y[32:40]] + [pltpu.roll(y[32:40], HEAD - 32 * g, 1) for g in range(1, 4)]
        steps = jnp.concatenate(steps, axis=0).T
        for t in range(STEPS // 2):
            decode_ref[2 * t + a] = steps[t * ROWS : (t + 1) * ROWS].astype(bf16)


def landing_kernel(row_ref, own_ref, far_ref, keys_ref, values_ref):
    group = lax.axis_index("group")
    owner = lax.axis_index(SEQ) * 2 + group
    blocks, tokens = SPAN // BLOCK, SPAN // 2
    row = row_ref[...]
    column = jnp.broadcast_to(row.astype(f32), (blocks, blocks)).T.astype(jnp.int32)
    earlier = lax.broadcasted_iota(jnp.int32, (blocks, blocks), 0) < lax.broadcasted_iota(
        jnp.int32, (blocks, blocks), 1
    )
    same = (column == row) & earlier
    rank = jnp.sum(jnp.where(same, 1.0, 0.0), axis=0, keepdims=True)
    code = jnp.broadcast_to(jnp.where(row == owner, rank, -1.0), (16, blocks)).astype(bf16)
    token = lax.broadcasted_iota(jnp.int32, (blocks, tokens), 1)
    block = lax.broadcasted_iota(jnp.int32, (blocks, tokens), 0)
    line = lax.broadcasted_iota(jnp.int32, (16, tokens), 0)
    place_in = lax.broadcasted_iota(jnp.int32, (16, tokens), 1) % BLOCK

    def picked(side, ref):
        spread = (token // 8) * 4 + side * 2 + (token % 8) // BLOCK == block
        codes = dot(code, jnp.where(spread, 1.0, 0.0).astype(bf16))
        chosen = (codes == (line // BLOCK).astype(f32)) & (place_in == line % BLOCK)
        x = ref[...].astype(f32).reshape(tokens, 2 * HEAD).astype(bf16)
        return dot(jnp.where(chosen, 1.0, 0.0).astype(bf16), x)

    y = picked(group, own_ref) + picked(1 - group, far_ref)
    keys_ref[...] = y[:, :HEAD].astype(bf16)
    values_ref[...] = y[:, HEAD:].astype(bf16)


def cost(flops, moved, exps=0):
    return pl.CostEstimate(flops=flops, bytes_accessed=moved, transcendentals=exps)


SMEM = pl.BlockSpec(memory_space=pltpu.SMEM)
VMEM = pl.BlockSpec(memory_space=pltpu.VMEM)


def near(x):
    return pltpu.with_memory_space_constraint(x, pltpu.VMEM)


def swap(x, axis):
    return lax.all_to_all(x, axis, 0, 0, tiled=True)


def body(
    prefill_queries,
    cached_keys,
    cached_values,
    span_keys,
    span_values,
    out_weight,
    decode_queries,
    decode_keys,
    decode_values,
    new_keys,
    new_values,
    request_lengths,
    row_requests,
    block_table,
):
    mine = jnp.concatenate([cached_keys, cached_values, span_keys, span_values], axis=0)
    far_weight = lax.ppermute(out_weight, "pair", [(0, 1), (1, 0)])
    other = lax.ppermute(mine, "group", [(0, 1), (1, 0)])

    lines = LOCAL * STEPS * ROWS
    decoded = pl.pallas_call(
        decode_kernel,
        name="decode",
        out_shape=jax.ShapeDtypeStruct((PEERS, 8, 3 * HEAD), bf16),
        in_specs=[SMEM] * 2 + [VMEM] * 5,
        out_specs=VMEM,
        scratch_shapes=[pltpu.VMEM((lines, HEAD), f32)] * 3 + [pltpu.VMEM((2 * STEPS * ROWS, HEAD), f32)] * 2,
        cost_estimate=cost(2 * 2 * 512 * SLOTS * HEAD * 8, 3 << 20, 512 * SLOTS),
    )(request_lengths, row_requests, decode_queries, decode_keys, decode_values, new_keys, new_values)

    packed = pl.pallas_call(
        prefill_kernel,
        name="prefill",
        out_shape=jax.ShapeDtypeStruct((MATES, 2, 8, WIDE), bf16),
        in_specs=[VMEM] * 7,
        out_specs=VMEM,
        scratch_shapes=[pltpu.VMEM((KEYS, HEAD), bf16), pltpu.VMEM((KEYS, 2 * HEAD), bf16)],
        cost_estimate=cost(4 * HALF * LOCAL * KEYS * HEAD, 4 << 20, HALF * LOCAL * KEYS),
    )(
        near(prefill_queries),
        near(cached_keys),
        near(cached_values),
        span_keys,
        span_values,
        near(other),
        decoded.reshape(MATES, 2, 8, 3 * HEAD),
    )

    packed, far_weight = lax.optimization_barrier((packed, far_weight))
    arrived = swap(packed.reshape(PEERS, 8, WIDE), SEQ)
    arrived, late_weight = lax.optimization_barrier((arrived, out_weight))
    attention, new_own = pl.pallas_call(
        combine_kernel,
        name="combine",
        out_shape=(
            jax.ShapeDtypeStruct((MATES, 8, THIN), bf16),
            jax.ShapeDtypeStruct((PEERS, 8, 2 * HEAD), bf16),
        ),
        in_specs=[VMEM],
        out_specs=(VMEM, VMEM),
        cost_estimate=cost(1 << 20, 2 << 20),
    )(near(arrived))
    new_far = lax.ppermute(new_own, "group", [(0, 1), (1, 0)])
    attention = swap(attention, SEQ[:2])
    landed_keys, landed_values = pl.pallas_call(
        landing_kernel,
        name="landing",
        out_shape=(jax.ShapeDtypeStruct((16, HEAD), bf16), jax.ShapeDtypeStruct((16, HEAD), bf16)),
        in_specs=[VMEM] * 3,
        out_specs=(VMEM, VMEM),
        cost_estimate=cost(1 << 22, 1 << 19),
    )(block_table.reshape(1, -1), near(new_own), near(new_far))
    attention, landed_keys, landed_values = lax.optimization_barrier((attention, landed_keys, landed_values))
    columns = out_weight.shape[1]
    near_weight = near(late_weight)
    partial = pl.pallas_call(
        project_kernel,
        name="project",
        out_shape=jax.ShapeDtypeStruct((16, columns // 8 + 8, HEAD), bf16),
        in_specs=[VMEM] * 3,
        out_specs=VMEM,
        scratch_shapes=[pltpu.VMEM(((HALF + STEPS * ROWS) // 2, STAT), f32)],
        cost_estimate=cost(2 * 320 * STAT * columns, 2 << 20),
    )(near(attention), near_weight, near(far_weight))
    partial = swap(partial, ("pair", "tensor"))
    prefill_out, decode_out = pl.pallas_call(
        last_kernel,
        name="last",
        out_shape=(
            jax.ShapeDtypeStruct((columns // 8, HALF), bf16),
            jax.ShapeDtypeStruct((STEPS, ROWS, columns // 8), bf16),
        ),
        in_specs=[VMEM],
        out_specs=(VMEM, VMEM),
        cost_estimate=cost(1 << 18, 1 << 19),
    )(near(partial))
    shape = (1, 4, BLOCK, HEAD)
    return (prefill_out.T, decode_out, landed_keys.reshape(shape), landed_values.reshape(shape))


def solution(mesh):
    torus = Mesh(
        mesh.devices.reshape(4, 4, 2, mesh.shape["tensor"], mesh.shape["group"]),
        (*SEQ, "tensor", "group"),
    )
    in_specs = (
        P(None, "tensor"),
        P(SEQ_GROUP, "tensor"),
        P(SEQ_GROUP, "tensor"),
        P(SEQ_GROUP, "tensor"),
        P(SEQ_GROUP, "tensor"),
        P("tensor", SEQ),
        P(None, "group", "tensor"),
        P("group", SEQ, "tensor"),
        P("group", SEQ, "tensor"),
        P(None, "group", "tensor"),
        P(None, "group", "tensor"),
        P(),
        P("group"),
        P(),
    )
    out_specs = (
        P("group", SEQ_TENSOR),
        P(None, "group", SEQ_TENSOR),
        P(SEQ_GROUP, None, None, "tensor"),
        P(SEQ_GROUP, None, None, "tensor"),
    )
    return jax.shard_map(body, mesh=torus, in_specs=in_specs, out_specs=out_specs, check_vma=False)
```

```python
import math

import jax
import jax.numpy as jnp
from jax import lax
from jax.experimental import pallas as pl
from jax.experimental.pallas import tpu as pltpu
from jax.sharding import Mesh
from jax.sharding import PartitionSpec as P


HEAD = 128
SPAN = 512
BLOCK = 4
STEPS = 4
SEQ = ("seq_0", "seq_1", "pair")
SEQ_GROUP = (*SEQ, "group")
SEQ_TENSOR = (*SEQ, "tensor")

PEERS = 32
MATES = PEERS // 2
LOCAL = 8
ROWS = 16
SLOTS = 256
CACHED = 1024
HALF = 256
KEYS = 2 * CACHED + 128
STAT = LOCAL * HEAD
DEC = STAT + HEAD
NEW = DEC + 2 * HEAD
WIDE = NEW + 2 * HEAD
THIN = STAT + 2 * HEAD
DEC_LANE = 32

NEG = -1e30
LOG2 = HEAD**-0.5 * math.log2(math.e)
bf16 = jnp.bfloat16
f32 = jnp.float32


def log_total(peak, total):
    safe = jnp.where(total > 0.0, total, 1.0)
    return jnp.where(total > 0.0, peak * LOG2 + jnp.log2(safe), NEG)


def terms(x):
    first = x.astype(bf16).astype(f32)
    rest = x - first
    second = rest.astype(bf16).astype(f32)
    return (first, second, rest - second)


def dot_t(a, b):
    return lax.dot_general(a, b, (((1,), (1,)), ((), ())), preferred_element_type=f32)


def dot(a, b):
    return lax.dot_general(a, b, (((1,), (0,)), ((), ())), preferred_element_type=f32)


def decode_kernel(lengths, requests, q_ref, k_ref, v_ref, nk_ref, nv_ref, out_ref, qs, os, ls, nks, nvs):
    lines = LOCAL * STEPS
    for h in range(LOCAL):
        for t in range(STEPS):
            at = (h * STEPS + t) * ROWS
            qs[at : at + ROWS, :] = q_ref[t, :, h * HEAD : (h + 1) * HEAD].astype(f32)
    for u in range(STEPS):
        nks[u * ROWS : (u + 1) * ROWS, :] = nk_ref[u].astype(f32)
        nvs[u * ROWS : (u + 1) * ROWS, :] = nv_ref[u].astype(f32)
    nks[STEPS * ROWS :, :] = jnp.zeros((STEPS * ROWS, HEAD), f32)
    nvs[STEPS * ROWS :, :] = jnp.zeros((STEPS * ROWS, HEAD), f32)
    seq = lax.axis_index(SEQ)
    position = seq * SLOTS + lax.broadcasted_iota(jnp.int32, (lines, SLOTS), 1)
    step = lax.broadcasted_iota(jnp.int32, (ROWS * lines, 8), 1)
    line_step = lax.broadcasted_iota(jnp.int32, (ROWS * lines, 8), 0) % STEPS
    step_seen = (step <= line_step) & (seq == 0)
    scores, step_scores, step_values = [], [], []
    for r in range(ROWS):
        q = qs[pl.ds(r, lines, stride=ROWS), :].astype(bf16)
        nk = nks[pl.ds(r, 8, stride=ROWS), :].astype(bf16)
        step_values.append(nvs[pl.ds(r, 8, stride=ROWS), :].astype(bf16))
        scores.append(jnp.where(position < lengths[requests[r]], dot_t(q, k_ref[r]), NEG))
        step_scores.append(dot_t(q, nk))
    s = jnp.concatenate(scores, axis=0)
    s2 = jnp.where(step_seen, jnp.concatenate(step_scores, axis=0), NEG)
    peak = jnp.maximum(jnp.max(s, axis=1, keepdims=True), jnp.max(s2, axis=1, keepdims=True))
    p = jnp.where(s > 0.5 * NEG, jnp.exp2((s - peak) * LOG2), 0.0)
    p2 = jnp.where(step_seen, jnp.exp2((s2 - peak) * LOG2), 0.0)
    total = jnp.sum(p, axis=1, keepdims=True) + jnp.sum(p2, axis=1, keepdims=True)
    p, p2 = p.astype(bf16), p2.astype(bf16)
    inverse = 1.0 / jnp.where(total > 0.0, total, 1.0)
    logs = log_total(peak, total)
    for r in range(ROWS):
        at = slice(r * lines, (r + 1) * lines)
        o = dot(p[at], v_ref[r]) + dot(p2[at], step_values[r])
        os[pl.ds(r, lines, stride=ROWS), :] = o * inverse[at]
        ls[pl.ds(r, lines, stride=ROWS), :] = jnp.broadcast_to(logs[at], (lines, HEAD))
    o = os[...].reshape(PEERS, 2, 8, HEAD)
    logs = ls[...].reshape(PEERS, 2, 8, HEAD)
    lane = lax.broadcasted_iota(jnp.int32, (PEERS, 8, HEAD), 2)
    stat = jnp.zeros((PEERS, 8, HEAD), f32)
    for b in range(2):
        out_ref[:, :, b * HEAD : (b + 1) * HEAD] = o[:, b].astype(bf16)
        for i, term in enumerate(terms(logs[:, b])):
            stat = jnp.where(lane == DEC_LANE + 3 * b + i, term, stat)
    out_ref[:, :, 2 * HEAD :] = stat.astype(bf16)


def prefill_kernel(q_ref, k_ref, v_ref, sk_ref, sv_ref, other_ref, dec_ref, out_ref, keys, values):
    seq, group = lax.axis_index(SEQ), lax.axis_index("group")
    own_k, own_v = sk_ref[...].astype(f32), sv_ref[...].astype(f32)
    far = other_ref[2 * CACHED :, :].astype(f32)
    far_k, far_v = far[:8], far[8:]
    first = jnp.full((8, HEAD), group, jnp.int32) == 0
    near_k = jnp.concatenate([jnp.where(first, own_k, far_k), jnp.where(first, far_k, own_k)], axis=0)
    near_v = jnp.concatenate([jnp.where(first, own_v, far_v), jnp.where(first, far_v, own_v)], axis=0)
    values[:, HEAD:] = jnp.ones((KEYS, HEAD), bf16)
    values[0:CACHED, 0:HEAD] = v_ref[...]
    values[CACHED : 2 * CACHED, 0:HEAD] = other_ref[CACHED : 2 * CACHED, :]
    keys[...] = jnp.zeros((HEAD, HEAD), bf16)
    values[2 * CACHED :, 0:HEAD] = jnp.zeros((HEAD, HEAD), bf16)
    keys[0:16, :] = near_k.astype(bf16)
    values[2 * CACHED : 2 * CACHED + 16, 0:HEAD] = near_v.astype(bf16)
    for a in range(2):
        out_ref[:, a, :, DEC:NEW] = dec_ref[:, a, :, 0 : 2 * HEAD]
        out_ref[:, a, :, NEW : NEW + HEAD] = jnp.broadcast_to(own_k[None], (MATES, 8, HEAD)).astype(bf16)
        out_ref[:, a, :, NEW + HEAD :] = jnp.broadcast_to(own_v[None], (MATES, 8, HEAD)).astype(bf16)

    lane = lax.broadcasted_iota(jnp.int32, (PEERS, 8, HEAD), 2)
    index = lax.broadcasted_iota(jnp.int32, (HALF, HEAD), 1)
    query = group * HALF + lax.broadcasted_iota(jnp.int32, (HALF, HEAD), 0)
    seen = (index < 16) & (seq * 16 + index <= query)
    mine = pl.ds(pl.multiple_of(group * HALF, HALF), HALF)

    def scores(h):
        q = q_ref[mine, h * HEAD : (h + 1) * HEAD]
        edge = jnp.where(seen, dot_t(q, keys[...]), NEG)
        return jnp.concatenate([dot_t(q, k_ref[...]), dot_t(q, other_ref[0:CACHED, :]), edge], axis=1)

    upcoming = scores(0)
    stat = jnp.concatenate([dec_ref[:, a, :, 2 * HEAD :].astype(f32) for a in range(2)], axis=0)
    for h in range(LOCAL):
        s = upcoming
        if h + 1 < LOCAL:
            upcoming = scores(h + 1)
        peak = jnp.max(s, axis=1, keepdims=True)
        edge = s[:, 2 * CACHED :]
        p = jnp.exp2((s[:, : 2 * CACHED] - peak) * LOG2)
        p = jnp.concatenate([p, jnp.where(seen, jnp.exp2((edge - peak) * LOG2), 0.0)], axis=1)
        o = dot(p.astype(bf16), values[...])
        o, total = o[:, :HEAD], o[:, HEAD:]
        o = (o / total).reshape(PEERS, 8, HEAD)
        for a in range(2):
            out_ref[:, a, :, h * HEAD : (h + 1) * HEAD] = o[a * MATES : (a + 1) * MATES].astype(bf16)
        logs = log_total(peak, total).reshape(PEERS, 8, HEAD)
        for i, term in enumerate(terms(logs)):
            stat = jnp.where(lane == 3 * h + i, term, stat)
    for a in range(2):
        out_ref[:, a, :, STAT:DEC] = stat[a * MATES : (a + 1) * MATES].astype(bf16)


def combine_kernel(in_ref, out_ref, new_ref):
    new_ref[...] = in_ref[:, :, NEW:]
    t = in_ref[:, :, STAT:DEC].astype(f32).reshape(PEERS * 8, HEAD)
    logs = t + pltpu.roll(t, HEAD - 1, 1) + pltpu.roll(t, HEAD - 2, 1)
    logs = logs.reshape(PEERS, 8, HEAD)
    share = jnp.exp2(logs - jnp.max(logs, axis=0)[None])
    share = share / jnp.sum(share, axis=0)[None]
    for j in range(LOCAL + 2):
        lane = 3 * j if j < LOCAL else DEC_LANE + 3 * (j - LOCAL)
        at = j * HEAD if j < LOCAL else DEC + (j - LOCAL) * HEAD
        x = in_ref[:, :, at : at + HEAD].astype(f32)
        total = jnp.sum(x * share[:, :, lane : lane + 1], axis=0)
        out_ref[:, :, j * HEAD : (j + 1) * HEAD] = jnp.broadcast_to(total[None], (MATES, 8, HEAD)).astype(bf16)


def project_kernel(in_ref, w_ref, far_ref, out_ref, rows):
    pair = lax.axis_index("pair")
    rows[0 : HALF // 2, :] = in_ref[:, :, 0:STAT].astype(f32).reshape(HALF // 2, STAT)
    for h in range(LOCAL):
        for t in range(STEPS // 2):
            for b in range(2):
                at = HALF // 2 + t * ROWS + b * 8
                x = in_ref[h * STEPS // 2 + t, :, STAT + b * HEAD : STAT + (b + 1) * HEAD]
                rows[at : at + 8, h * HEAD : (h + 1) * HEAD] = x.astype(f32)
    x = rows[...].astype(bf16)

    for ref, side in ((w_ref, pair), (far_ref, 1 - pair)):
        y = dot(x, ref[...])
        y = jnp.concatenate([y, jnp.zeros((2 * HEAD - y.shape[0], y.shape[1]), f32)], axis=0)
        y = y.astype(bf16).T
        steps = y[:, HEAD:].astype(f32).reshape(8, 4, 8, HEAD)
        packed = steps[:, 0].reshape(8 * 8, HEAD) + sum(pltpu.roll(steps[:, g].reshape(8 * 8, HEAD), 32 * g, 1) for g in range(1, 4))
        peers = pl.ds(pl.multiple_of(side * 8, 8), 8)
        out_ref[peers, 0:32, :] = y[:, :HEAD].reshape(8, 32, HEAD)
        out_ref[peers, 32:40, :] = packed.reshape(8, 8, HEAD).astype(bf16)


def last_kernel(in_ref, prefill_ref, decode_ref):
    for a in range(2):
        y = jnp.sum(in_ref[a * 8 : (a + 1) * 8].astype(f32), axis=0)
        prefill_ref[:, a * HEAD : (a + 1) * HEAD] = y[0:32].astype(bf16)
        steps = [y[32:40]] + [pltpu.roll(y[32:40], HEAD - 32 * g, 1) for g in range(1, 4)]
        steps = jnp.concatenate(steps, axis=0).T
        for t in range(STEPS // 2):
            decode_ref[2 * t + a] = steps[t * ROWS : (t + 1) * ROWS].astype(bf16)


def landing_kernel(row_ref, own_ref, far_ref, keys_ref, values_ref):
    group = lax.axis_index("group")
    owner = lax.axis_index(SEQ) * 2 + group
    blocks, tokens = SPAN // BLOCK, SPAN // 2
    row = row_ref[...]
    column = jnp.broadcast_to(row.astype(f32), (blocks, blocks)).T.astype(jnp.int32)
    earlier = lax.broadcasted_iota(jnp.int32, (blocks, blocks), 0) < lax.broadcasted_iota(
        jnp.int32, (blocks, blocks), 1
    )
    same = (column == row) & earlier
    rank = jnp.sum(jnp.where(same, 1.0, 0.0), axis=0, keepdims=True)
    code = jnp.broadcast_to(jnp.where(row == owner, rank, -1.0), (16, blocks)).astype(bf16)
    token = lax.broadcasted_iota(jnp.int32, (blocks, tokens), 1)
    block = lax.broadcasted_iota(jnp.int32, (blocks, tokens), 0)
    line = lax.broadcasted_iota(jnp.int32, (16, tokens), 0)
    place_in = lax.broadcasted_iota(jnp.int32, (16, tokens), 1) % BLOCK

    def picked(side, ref):
        spread = (token // 8) * 4 + side * 2 + (token % 8) // BLOCK == block
        codes = dot(code, jnp.where(spread, 1.0, 0.0).astype(bf16))
        chosen = (codes == (line // BLOCK).astype(f32)) & (place_in == line % BLOCK)
        x = ref[...].astype(f32).reshape(tokens, 2 * HEAD).astype(bf16)
        return dot(jnp.where(chosen, 1.0, 0.0).astype(bf16), x)

    y = picked(group, own_ref) + picked(1 - group, far_ref)
    keys_ref[...] = y[:, :HEAD].astype(bf16)
    values_ref[...] = y[:, HEAD:].astype(bf16)


def cost(flops, moved, exps=0):
    return pl.CostEstimate(flops=flops, bytes_accessed=moved, transcendentals=exps)


SMEM = pl.BlockSpec(memory_space=pltpu.SMEM)
VMEM = pl.BlockSpec(memory_space=pltpu.VMEM)


def near(x):
    return pltpu.with_memory_space_constraint(x, pltpu.VMEM)


def swap(x, axis):
    return lax.all_to_all(x, axis, 0, 0, tiled=True)


def body(
    prefill_queries,
    cached_keys,
    cached_values,
    span_keys,
    span_values,
    out_weight,
    decode_queries,
    decode_keys,
    decode_values,
    new_keys,
    new_values,
    request_lengths,
    row_requests,
    block_table,
):
    mine = jnp.concatenate([cached_keys, cached_values, span_keys, span_values], axis=0)
    far_weight = lax.ppermute(out_weight, "pair", [(0, 1), (1, 0)])
    other = lax.ppermute(mine, "group", [(0, 1), (1, 0)])

    lines = LOCAL * STEPS * ROWS
    decoded = pl.pallas_call(
        decode_kernel,
        name="decode",
        out_shape=jax.ShapeDtypeStruct((PEERS, 8, 3 * HEAD), bf16),
        in_specs=[SMEM] * 2 + [VMEM] * 5,
        out_specs=VMEM,
        scratch_shapes=[pltpu.VMEM((lines, HEAD), f32)] * 3 + [pltpu.VMEM((2 * STEPS * ROWS, HEAD), f32)] * 2,
        cost_estimate=cost(2 * 2 * 512 * SLOTS * HEAD * 8, 3 << 20, 512 * SLOTS),
    )(request_lengths, row_requests, decode_queries, decode_keys, decode_values, new_keys, new_values)

    packed = pl.pallas_call(
        prefill_kernel,
        name="prefill",
        out_shape=jax.ShapeDtypeStruct((MATES, 2, 8, WIDE), bf16),
        in_specs=[VMEM] * 7,
        out_specs=VMEM,
        scratch_shapes=[pltpu.VMEM((HEAD, HEAD), bf16), pltpu.VMEM((KEYS, 2 * HEAD), bf16)],
        cost_estimate=cost(4 * HALF * LOCAL * KEYS * HEAD, 4 << 20, HALF * LOCAL * KEYS),
    )(
        near(prefill_queries),
        near(cached_keys),
        near(cached_values),
        span_keys,
        span_values,
        near(other),
        decoded.reshape(MATES, 2, 8, 3 * HEAD),
    )

    packed, far_weight = lax.optimization_barrier((packed, far_weight))
    arrived = swap(packed.reshape(PEERS, 8, WIDE), SEQ)
    arrived, late_weight = lax.optimization_barrier((arrived, out_weight))
    attention, new_own = pl.pallas_call(
        combine_kernel,
        name="combine",
        out_shape=(
            jax.ShapeDtypeStruct((MATES, 8, THIN), bf16),
            jax.ShapeDtypeStruct((PEERS, 8, 2 * HEAD), bf16),
        ),
        in_specs=[VMEM],
        out_specs=(VMEM, VMEM),
        cost_estimate=cost(1 << 20, 2 << 20),
    )(near(arrived))
    new_far = lax.ppermute(new_own, "group", [(0, 1), (1, 0)])
    attention = swap(attention, SEQ[:2])
    landed_keys, landed_values = pl.pallas_call(
        landing_kernel,
        name="landing",
        out_shape=(jax.ShapeDtypeStruct((16, HEAD), bf16), jax.ShapeDtypeStruct((16, HEAD), bf16)),
        in_specs=[VMEM] * 3,
        out_specs=(VMEM, VMEM),
        cost_estimate=cost(1 << 22, 1 << 19),
    )(block_table.reshape(1, -1), near(new_own), near(new_far))
    attention, landed_keys, landed_values = lax.optimization_barrier((attention, landed_keys, landed_values))
    columns = out_weight.shape[1]
    near_weight = near(late_weight)
    partial = pl.pallas_call(
        project_kernel,
        name="project",
        out_shape=jax.ShapeDtypeStruct((16, columns // 8 + 8, HEAD), bf16),
        in_specs=[VMEM] * 3,
        out_specs=VMEM,
        scratch_shapes=[pltpu.VMEM(((HALF + STEPS * ROWS) // 2, STAT), f32)],
        cost_estimate=cost(2 * 320 * STAT * columns, 2 << 20),
    )(near(attention), near_weight, near(far_weight))
    partial = swap(partial, ("pair", "tensor"))
    prefill_out, decode_out = pl.pallas_call(
        last_kernel,
        name="last",
        out_shape=(
            jax.ShapeDtypeStruct((columns // 8, HALF), bf16),
            jax.ShapeDtypeStruct((STEPS, ROWS, columns // 8), bf16),
        ),
        in_specs=[VMEM],
        out_specs=(VMEM, VMEM),
        cost_estimate=cost(1 << 18, 1 << 19),
    )(near(partial))
    shape = (1, 4, BLOCK, HEAD)
    return (prefill_out.T, decode_out, landed_keys.reshape(shape), landed_values.reshape(shape))


def solution(mesh):
    torus = Mesh(
        mesh.devices.reshape(4, 4, 2, mesh.shape["tensor"], mesh.shape["group"]),
        (*SEQ, "tensor", "group"),
    )
    in_specs = (
        P(None, "tensor"),
        P(SEQ_GROUP, "tensor"),
        P(SEQ_GROUP, "tensor"),
        P(SEQ_GROUP, "tensor"),
        P(SEQ_GROUP, "tensor"),
        P("tensor", SEQ),
        P(None, "group", "tensor"),
        P("group", SEQ, "tensor"),
        P("group", SEQ, "tensor"),
        P(None, "group", "tensor"),
        P(None, "group", "tensor"),
        P(),
        P("group"),
        P(),
    )
    out_specs = (
        P("group", SEQ_TENSOR),
        P(None, "group", SEQ_TENSOR),
        P(SEQ_GROUP, None, None, "tensor"),
        P(SEQ_GROUP, None, None, "tensor"),
    )
    return jax.shard_map(body, mesh=torus, in_specs=in_specs, out_specs=out_specs, check_vma=False)
```
